128 devices in a mesh: rep: 4 (over x_hi, core), own: 32 (over x_lo, z, y).
Axes of the slice: x: 4 (x_hi: 2, x_lo: 2; x = x_hi * 2 + x_lo), y: 4, z: 4, core: 2. Of those that a mesh axis runs over, the one named last changes fastest.
Arguments:
- replica_delta: float32 [4, 32, 256, 1792], P('rep', None, 'own'), may hold values from -6 to 6
- layer_basis: float32 [4, 1792, 64], replicated, may hold values from -0.25 to 0.25
- layer_of: int32 [32], replicated, may hold values from 0 to 3
- owner_of: int32 [32], replicated, may hold values from 0 to 31, as said below
- weights_owned: float32 [64, 256, 1792], P('own'), may hold values from -6 to 6
- momentum_owned: float32 [64, 256, 1792], P('own'), may hold values from -4 to 4
Outputs:
- new_weights: float32 [64, 256, 1792], P('own')
- new_momentum: float32 [64, 256, 1792], P('own')
- replica_weights: float32 [32, 256, 1792], P(None, 'own')
The draws below stay inside these ranges and needn't reach their ends.
Inputs may be any that keep to these rules, and one draw needn't show every extreme that they name: `owner_of`: no owner holds more than 2 blocks, and some owner holds exactly 2; the slots of an owner are taken in the order of the blocks.
All inputs are finite; a program needn't handle non-finite values.
Results may differ from the reference program's by a relative error of at most 0.00007.
Values sent between devices are 32-bit elements; how exact they have to be, the bound alone decides.
A program may use at most 128 MiB of HBM per device.

```python
import jax
import jax.numpy as jnp
from jax import lax

D = 1792
RANK = 64
LAYERS = 4
CAP = 2
ROWS = 256
BLOCKS = 32
SLOTS = 64
N_REP = 4
N_OWN = 32


def draw_owner_of(key, part):
    first_key, order_key, shuffle_key = jax.random.split(key, 3)
    slot_total = N_OWN * CAP
    favoured = jax.random.randint(first_key, (), 0, N_OWN)
    slot_order = jax.random.permutation(order_key, slot_total)
    position = jnp.zeros((slot_total,), jnp.int32).at[slot_order].set(jnp.arange(slot_total, dtype=jnp.int32))
    slot_index = jnp.arange(slot_total, dtype=jnp.int32)
    slot_score = jnp.where(slot_index // CAP == favoured, slot_index % CAP - CAP, position)
    picked = jnp.argsort(slot_score, stable=True)[:BLOCKS]
    owners = (picked // CAP).astype(jnp.int32)
    return owners[jax.random.permutation(shuffle_key, BLOCKS)]


def with_ends(array, rng, low, high):
    place = [jax.random.randint(jax.random.fold_in(rng, axis), (), 0, length) for axis, length in enumerate(array.shape)]
    main_axis = array.shape.index(max(array.shape))
    next_to = place[:main_axis] + [(place[main_axis] + 1) % array.shape[main_axis]] + place[main_axis + 1:]
    return array.at[tuple(place)].set(low).at[tuple(next_to)].set(high)


def steps_of(rng, extent, cuts, least, largest):
    level = 1.0
    for dim, parts in cuts:
        draws = jax.random.uniform(jax.random.fold_in(jax.random.fold_in(rng, 6), dim), (parts,), jnp.float32, least / len(cuts), largest / len(cuts))
        level = level * jnp.repeat(jnp.exp(draws), extent[dim] // parts).reshape((-1,) + (1,) * (len(extent) - 1 - dim))
    return level


def gaussian(rng, shape, scale, bound, shards=(), kind=jnp.bfloat16):
    values = jax.random.normal(rng, shape, jnp.float32) * scale
    if len(shards) > 0:
        values = steps_of(rng, shape, shards, -0.22, 0.18) * values
    return jnp.clip(values, min=-bound, max=bound).astype(kind)


def setup_inputs(seed: int = 0) -> dict:
    keys = jax.random.split(jax.random.key(seed), 7)
    replica_delta = gaussian(keys[0], (N_REP, BLOCKS, ROWS, D), 1.0, 6.0, ((0, 4), (2, 32)), jnp.float32)
    layer_basis = gaussian(keys[1], (LAYERS, D, RANK), (8 * RANK) ** -0.5, 0.25, (), jnp.float32)
    layer_of = with_ends(jax.random.randint(keys[2], (BLOCKS,), 0, LAYERS), jax.random.fold_in(keys[2], 1), 0, LAYERS - 1).astype(jnp.int32)
    owner_of = draw_owner_of(jax.random.fold_in(keys[6], 71), 0)
    weights_owned = gaussian(keys[4], (SLOTS, ROWS, D), 1.0, 6.0, ((0, 32),), jnp.float32)
    momentum_owned = gaussian(keys[5], (SLOTS, ROWS, D), 0.3, 4.0, ((0, 32),), jnp.float32)
    return dict(replica_delta=replica_delta, layer_basis=layer_basis, layer_of=layer_of, owner_of=owner_of, weights_owned=weights_owned, momentum_owned=momentum_owned)


momentum_decay = 0.9
outer_rate = 0.7


def reference(replica_delta, layer_basis, layer_of, owner_of, weights_owned, momentum_owned):
    highest = lax.Precision.HIGHEST
    blocks = owner_of.shape[0]
    same_owner = owner_of[None, :] == owner_of[:, None]
    positions = jnp.arange(blocks, dtype=jnp.int32)
    earlier = positions[None, :] < positions[:, None]
    rank_in = jnp.sum((same_owner & earlier).astype(jnp.int32), axis=1).astype(jnp.int32)
    slot_of = (owner_of * CAP + rank_in).astype(jnp.int32)
    chosen = layer_basis[layer_of.astype(jnp.int32)]
    coeffs = jnp.einsum("rbnd,bdk->rbnk", replica_delta, chosen, precision=highest)
    averaged = jnp.sum(coeffs, axis=0) / N_REP
    outer_grad = jnp.einsum("bnk,bdk->bnd", averaged, chosen, precision=highest)
    slot_total = weights_owned.shape[0]
    holding = (slot_of[None, :] == jnp.arange(slot_total, dtype=jnp.int32)[:, None]).astype(jnp.float32)
    outer_slot = jnp.einsum("sb,bnd->snd", holding, outer_grad, precision=highest)
    in_use = jnp.sum(holding, axis=1)[:, None, None]
    new_momentum = (momentum_decay * momentum_owned + outer_slot) * in_use
    new_weights = (weights_owned - outer_rate * (outer_slot + momentum_decay * new_momentum)) * in_use
    replica_weights = new_weights[slot_of]
    return new_weights, new_momentum, replica_weights
```

```python
import functools

import jax
import jax.numpy as jnp
from jax import lax
from jax.experimental import pallas as pl
from jax.experimental.pallas import tpu as pltpu
from jax.sharding import PartitionSpec as P

momentum_decay = 0.9
outer_rate = 0.7

MESH = pl.DeviceIdType.MESH
HIGHEST = lax.Precision.HIGHEST
D = 1792
HALF = D // 2
RANK = 64
BLOCKS = 32
OWN = 32
TILE = 256

FAR = [(1, 2), (3, 2), (2, 1), (2, 3), (1, 1), (3, 3), (1, 3), (3, 1), (2, 2),
       (2, 0), (0, 2), (1, 0), (0, 1), (3, 0), (0, 3)]


def place():
    rep = lax.axis_index("rep")
    own = lax.axis_index("own")
    x = (rep // 2) * 2 + own // 16
    return x, own % 4, (own // 4) % 4, rep % 2


def device(x, y, z, core):
    return ((x // 2) * 2 + core, (x % 2) * 16 + z * 4 + y)


def send(src, dst, send_sem, recv_sem, to):
    return pltpu.make_async_remote_copy(
        src_ref=src, dst_ref=dst, send_sem=send_sem, recv_sem=recv_sem,
        device_id=to, device_id_type=MESH,
    )


def kernel(
    owner_s, owner_v, layer_v, delta_hbm, basis_hbm, weights_hbm, momentum_hbm,
    new_weights, new_momentum, replica,
    w, m, d, bt, q, r, relay, og, part, part_sum, from_core, from_x, packed, placed,
    slots,
    load_sem, near_send, near_recv, far_send, far_recv, relay_send, relay_recv,
    side_send, side_recv, swap_send, swap_recv, packed_send, packed_recv, own_sem,
):
    x, y, z, core = place()
    lo, hi = x % 2, x // 2
    me = lo * 16 + z * 4 + y
    other = 1 - core
    x_up, x_down, x_far = (x + 1) % 4, (x + 3) % 4, (x + 2) % 4
    up, down = device(x_up, y, z, core), device(x_down, y, z, core)
    partner, opposite = device(x, y, z, other), device(x_far, y, z, core)

    mine = pl.ds(pl.multiple_of(core * HALF, 128), HALF)
    rest = pl.ds(pl.multiple_of(other * HALF, 128), HALF)
    loads = [
        (weights_hbm.at[:, :, :, mine], w.at[:, :, :, mine]),
        (momentum_hbm.at[:, :, :, mine], m.at[:, :, :, mine]),
        (delta_hbm, d),
        (basis_hbm, bt),
        (weights_hbm.at[:, :, :, rest], w.at[:, :, :, rest]),
        (momentum_hbm.at[:, :, :, rest], m.at[:, :, :, rest]),
    ]
    copies = [pltpu.make_async_copy(a, b, load_sem.at[i]) for i, (a, b) in enumerate(loads)]
    for copy in copies:
        copy.start()

    barrier = pltpu.get_barrier_semaphore()
    count = 0
    for dy, dz in FAR:
        for side in range(2):
            to = device((1 - side) * x + side * (hi * 2 + 1 - lo), (y + dy) % 4, (z + dz) % 4, core)
            pl.semaphore_signal(barrier, inc=1, device_id=to, device_id_type=MESH)
            count += 1
    for to in (up, down, partner, opposite):
        pl.semaphore_signal(barrier, inc=1, device_id=to, device_id_type=MESH)
        count += 1

    def slot_body(b, carry):
        owner = owner_s[b]
        rank = lax.fori_loop(
            0, BLOCKS, lambda e, t: t + jnp.where((owner_s[e] == owner) & (e < b), 1, 0), 0
        )
        slots[b] = owner * 2 + rank
        return carry

    copies[0].wait()
    copies[1].wait()

    def q_body(o, carry):
        for half in range(2):
            @pl.when(core == half)
            def _():
                cols = slice(half * HALF, (half + 1) * HALF)
                for s in range(2):
                    q[o, s] = w[s, o, :, cols] - (outer_rate * momentum_decay * momentum_decay) * m[s, o, :, cols]
        return carry

    lax.fori_loop(0, OWN, q_body, 0)
    lax.fori_loop(0, BLOCKS, slot_body, 0)

    pl.semaphore_wait(barrier, count)

    def far_copies(i):
        dy, dz = FAR[i]
        ty, tz = (y + dy) % 4, (z + dz) % 4
        to = device(x, ty, tz, core)
        direct = send(q.at[lo * 16 + tz * 4 + ty], r.at[core, me], far_send, far_recv.at[i], to)
        onward = send(
            q.at[(1 - lo) * 16 + tz * 4 + ty, hi], relay.at[z * 4 + y], relay_send, relay_recv.at[i], to
        )
        return direct, onward

    own_copy = pltpu.make_async_copy(q.at[me], r.at[core, me], own_sem.at[0])
    own_copy.start()
    own_swap = send(q.at[me], r.at[core, me], swap_send, swap_recv.at[15], partner)
    own_swap.start()
    across = (1 - lo) * 16 + z * 4 + y
    side = [
        send(q.at[across, hi], r.at[core, me, hi], side_send, side_recv.at[0, 15], up),
        send(q.at[across, hi], r.at[core, me, hi], side_send, side_recv.at[1, 15], down),
    ]
    for copy in side:
        copy.start()
    far = [far_copies(i) for i in range(15)]
    first = 8
    for direct, onward in far[:first]:
        onward.start()
        direct.start()

    row = lax.broadcasted_iota(jnp.int32, (256, 1), 0)
    lane256 = lax.broadcasted_iota(jnp.int32, (1, 256), 1)
    lane128 = lax.broadcasted_iota(jnp.int32, (1, 128), 1)
    lane32 = lax.broadcasted_iota(jnp.int32, (1, BLOCKS), 1)
    layer_row = layer_v[...]
    owner_row = owner_v[...]
    layer_col = jnp.sum(jnp.where(row // 8 == lane32, layer_row, 0), axis=1, keepdims=True)
    in_layer = (lane256 // RANK) == layer_col
    low = lane128 < RANK

    copies[2].wait()
    copies[3].wait()
    every = lax.dot_general(
        d[...], bt[...], (((1,), (1,)), ((), ())), precision=HIGHEST,
        preferred_element_type=jnp.float32,
    )
    every = jnp.where(in_layer, every, 0.0)
    both = every[:, :128] + every[:, 128:]
    both = both + pltpu.roll(both, RANK, 1)
    part[...] = jnp.where(low, both[:128], both[128:])
    core_copy = send(part, from_core, packed_send.at[0], packed_recv.at[0], partner)
    core_copy.start()

    blk_col = lax.broadcasted_iota(jnp.int32, (BLOCKS, 1), 0)
    owner_col = jnp.sum(jnp.where(blk_col == lane32, owner_row, 0), axis=1, keepdims=True)
    rank_col = jnp.sum(
        jnp.where((owner_col == owner_row) & (lane32 < blk_col), 1, 0), axis=1, keepdims=True
    )
    slot_col = owner_col * 2 + rank_col
    layer_blk = jnp.sum(jnp.where(blk_col == lane32, layer_row, 0), axis=1, keepdims=True)
    slot_lane = jnp.sum(jnp.where(lane256 // 8 == blk_col, slot_col, 0), axis=0, keepdims=True)
    same_row = (row % 8) == (lane256 % 8)
    pick = [
        jnp.where(((row // 8) * 2 + j == slot_lane) & same_row, 1.0, 0.0) for j in range(2)
    ]
    used, layers = [], []
    for j in range(2):
        hit = slot_col == me * 2 + j
        used.append(jnp.sum(jnp.where(hit, 1.0, 0.0), axis=0, keepdims=True))
        layers.append(jnp.sum(jnp.where(hit, layer_blk, 0), axis=0, keepdims=True))

    core_copy.wait()
    part_sum[...] = part[...] + from_core[...]
    x_copy = send(part_sum, from_x, packed_send.at[1], packed_recv.at[1], opposite)
    x_copy.start()
    x_copy.wait()
    averaged = (part_sum[...] + from_x[...]) * 0.25
    turned = pltpu.roll(averaged, RANK, 1)
    dup = jnp.concatenate(
        [jnp.where(low, averaged, turned), jnp.where(low, turned, averaged)], axis=0
    )
    chosen = [
        jnp.dot(p, dup, precision=HIGHEST, preferred_element_type=jnp.float32) for p in pick
    ]
    packed[...] = jnp.where(low, chosen[0], chosen[1]).reshape(OWN, 8, 128)

    def spread(pairs, keep):
        return jnp.where(keep, jnp.concatenate([pairs, pairs], axis=1), 0.0)

    og_coeffs = spread(dup, in_layer)

    own_packed = pltpu.make_async_copy(packed.at[me], placed.at[me], own_sem.at[1])
    own_packed.start()
    for dy, dz in [(0, 0)] + FAR:
        for s in range(2):
            if s == 0 and (dy, dz) == (0, 0):
                continue
            ty, tz = (y + dy) % 4, (z + dz) % 4
            to_lo = lo if s == 0 else 1 - lo
            send(
                packed.at[to_lo * 16 + tz * 4 + ty], placed.at[me], packed_send.at[2],
                packed_recv.at[2], device(hi * 2 + to_lo, ty, tz, core),
            ).start()
    for direct, onward in far[first:]:
        onward.start()
        direct.start()

    def og_body(j, carry):
        cols = pl.ds(pl.multiple_of(j * TILE, TILE), TILE)
        og[:, cols] = jnp.dot(
            og_coeffs, bt[:, cols], precision=HIGHEST, preferred_element_type=jnp.float32
        )
        return carry

    lax.fori_loop(0, D // TILE, og_body, 0)

    def onward_step(i):
        dy, dz = FAR[i]
        fy, fz = (y + 4 - dy) % 4, (z + 4 - dz) % 4
        src = lo * 16 + fz * 4 + fy
        far[i][1].wait_recv()
        for k, to in enumerate((up, down)):
            send(relay.at[fz * 4 + fy], r.at[core, src, hi], side_send, side_recv.at[k, i], to).start()

    def swap_step(i):
        dy, dz = FAR[i]
        fy, fz = (y + 4 - dy) % 4, (z + 4 - dz) % 4
        src = lo * 16 + fz * 4 + fy
        far[i][0].wait_recv()
        send(r.at[core, src], r.at[core, src], swap_send, swap_recv.at[i], partner).start()

    def side_step(i):
        dy, dz = FAR[i] if i < 15 else (0, 0)
        fy, fz = (y + 4 - dy) % 4, (z + 4 - dz) % 4
        src = (1 - lo) * 16 + fz * 4 + fy
        hi_down, hi_up = x_down // 2, x_up // 2
        send(relay.at[0], r.at[core, src, hi_down], side_send, side_recv.at[0, i], up).wait_recv()
        send(relay.at[0], r.at[core, src, hi_up], side_send, side_recv.at[1, i], down).wait_recv()
        send(r.at[core, src], r.at[core, src], swap_send, swap_recv.at[16 + i], partner).start()

    for i in range(first):
        onward_step(i)
        swap_step(i)

    own_packed.wait()
    send(packed.at[pl.ds(0, 31)], placed.at[pl.ds(0, 31)], packed_send.at[2], packed_recv.at[2], up).wait_recv()
    copies[4].wait()
    copies[5].wait()
    got = placed[...].reshape(256, 128)
    got_turned = pltpu.roll(got, RANK, 1)
    for j in range(2):
        pairs = jnp.where(low, got, got_turned) if j == 0 else jnp.where(low, got_turned, got)
        coeffs = spread(pairs, jnp.broadcast_to((lane256 // RANK) == layers[j], (256, 256)))
        use = used[j]

        def owner_body(t, carry, j=j, coeffs=coeffs, use=use):
            cols = pl.ds(pl.multiple_of(t * TILE, TILE), TILE)
            grad = jnp.dot(
                coeffs, bt[:, cols], precision=HIGHEST, preferred_element_type=jnp.float32
            ) * use
            grad = grad.reshape(OWN, 8, TILE)
            moved = (momentum_decay * m[j, :, :, cols] + grad) * use
            new_momentum[j, :, :, cols] = moved
            new_weights[j, :, :, cols] = (
                w[j, :, :, cols] - outer_rate * (grad + momentum_decay * moved)
            ) * use
            return carry

        lax.fori_loop(0, D // TILE, owner_body, 0)

    for i in range(first, 15):
        onward_step(i)
        swap_step(i)
    side_step(15)
    for i in range(15):
        side_step(i)

    own_copy.wait()
    for i in range(32):
        send(r.at[0, 0], r.at[other, 0], swap_send, swap_recv.at[i], partner).wait_recv()

    def out_body(b, carry):
        slot = slots[b]
        for half in range(2):
            cols = slice(half * HALF, (half + 1) * HALF)
            replica[b, :, cols] = r[half, slot // 2, slot % 2] - (
                outer_rate * (1.0 + momentum_decay)
            ) * og[pl.ds(pl.multiple_of(b * 8, 8), 8), cols]
        return carry

    lax.fori_loop(0, BLOCKS, out_body, 0)

    send(q.at[pl.ds(0, 15)], q.at[pl.ds(0, 15)], far_send, far_recv.at[0], up).wait_send()
    send(relay.at[pl.ds(0, 15)], relay.at[pl.ds(0, 15)], relay_send, far_recv.at[0], up).wait_send()
    send(q.at[pl.ds(0, 16)], q.at[pl.ds(0, 16)], side_send, far_recv.at[0], up).wait_send()
    send(q, q, swap_send, far_recv.at[0], up).wait_send()
    send(packed.at[pl.ds(0, 31)], placed.at[pl.ds(0, 31)], packed_send.at[2], packed_recv.at[2], up).wait_send()


def local(replica_delta, layer_basis, layer_of, owner_of, weights_owned, momentum_owned):
    vmem = pl.BlockSpec(memory_space=pltpu.VMEM)
    smem = pl.BlockSpec(memory_space=pltpu.SMEM)
    hbm = pl.BlockSpec(memory_space=pl.ANY)
    dma = pltpu.SemaphoreType.DMA
    f32 = jnp.float32
    basis = jnp.swapaxes(layer_basis, 1, 2).reshape(4 * RANK, D)
    delta = replica_delta.reshape(256, D)
    weights = weights_owned.reshape(2, OWN, 8, D)
    momentum = momentum_owned.reshape(2, OWN, 8, D)
    new_weights, new_momentum, replica = pl.pallas_call(
        kernel,
        out_shape=(
            pltpu.VMEM((2, OWN, 8, D), f32),
            pltpu.VMEM((2, OWN, 8, D), f32),
            pltpu.VMEM((BLOCKS, 8, D), f32),
        ),
        in_specs=[smem, vmem, vmem, hbm, hbm, hbm, hbm],
        out_specs=(vmem, vmem, vmem),
        scratch_shapes=[
            pltpu.VMEM((2, OWN, 8, D), f32),
            pltpu.VMEM((2, OWN, 8, D), f32),
            pltpu.VMEM((256, D), f32),
            pltpu.VMEM((256, D), f32),
            pltpu.VMEM((OWN, 2, 8, HALF), f32),
            pltpu.VMEM((2, OWN, 2, 8, HALF), f32),
            pltpu.VMEM((16, 8, HALF), f32),
            pltpu.VMEM((256, D), f32),
            pltpu.VMEM((128, 128), f32),
            pltpu.VMEM((128, 128), f32),
            pltpu.VMEM((128, 128), f32),
            pltpu.VMEM((128, 128), f32),
            pltpu.VMEM((OWN, 8, 128), f32),
            pltpu.VMEM((OWN, 8, 128), f32),
            pltpu.SMEM((BLOCKS,), jnp.int32),
            dma((6,)),
            dma, dma,
            dma, dma((15,)),
            dma, dma((15,)),
            dma, dma((2, 16)),
            dma, dma((32,)),
            dma((3,)), dma((3,)),
            dma((2,)),
        ],
        compiler_params=pltpu.CompilerParams(
            collective_id=0, has_side_effects=True, vmem_limit_bytes=48 << 20
        ),
        name="outer_step",
    )(
        owner_of, owner_of.reshape(1, BLOCKS), layer_of.reshape(1, BLOCKS),
        delta, basis, weights, momentum,
    )
    return (
        new_weights.reshape(2, 256, D),
        new_momentum.reshape(2, 256, D),
        replica,
    )


def solution(mesh):
    placed = (
        P("rep", None, "own", None),
        P(),
        P(),
        P(),
        P("own", None, None),
        P("own", None, None),
    )
    return jax.shard_map(
        local,
        mesh=mesh,
        in_specs=placed,
        out_specs=(P("own", None, None), P("own", None, None), P(None, "own", None)),
        check_vma=False,
    )
```

```python
import jax
import jax.numpy as jnp
from jax import lax
from jax.experimental import pallas as pl
from jax.experimental.pallas import tpu as pltpu
from jax.sharding import PartitionSpec as P

momentum_decay = 0.9
outer_rate = 0.7

MESH = pl.DeviceIdType.MESH
HIGHEST = lax.Precision.HIGHEST
D = 1792
HALF = D // 2
RANK = 64
BLOCKS = 32
OWN = 32
TILE = 256
BF16 = jnp.bfloat16
F32 = jnp.float32

DZ = [0, 1, 3, 2]
NEAR = [(1, 0), (3, 0), (2, 0)] + [(dy, dz) for dz in DZ[1:] for dy in (0, 1, 3, 2)]
FAR = [(1, 2), (3, 2), (2, 1), (2, 3), (1, 1), (3, 3), (1, 3), (3, 1), (2, 2),
       (2, 0), (0, 2), (1, 0), (0, 1), (3, 0), (0, 3)]
FIRST = 6


def place():
    rep = lax.axis_index("rep")
    own = lax.axis_index("own")
    x = (rep // 2) * 2 + own // 16
    return x, own % 4, (own // 4) % 4, rep % 2


def device(x, y, z, core):
    return ((x // 2) * 2 + core, (x % 2) * 16 + z * 4 + y)


def send(src, dst, send_sem, recv_sem, to):
    return pltpu.make_async_remote_copy(
        src_ref=src, dst_ref=dst, send_sem=send_sem, recv_sem=recv_sem,
        device_id=to, device_id_type=MESH,
    )


def split(value):
    high = value.astype(BF16)
    return high, (value - high.astype(F32)).astype(BF16)


def dot(a, b, dims=((1,), (0,))):
    return lax.dot_general(a, b, (dims, ((), ())), preferred_element_type=F32)


def exchange(
    owner_hbm, layer_hbm, delta_hbm, basis_hbm, weights_hbm, momentum_hbm,
    new_weights, new_momentum, r, og, slots,
    owner_v, layer_v, w, m, d, bt, bt_high, bt_low, q, relay, parts, packed, placed,
    load_sem, far_send, far_recv, relay_send, relay_recv, side_send, side_recv,
    swap_send, swap_recv, part_send, part_recv, packed_send, packed_recv, own_sem,
    table_sem,
):
    x, y, z, core = place()
    lo, hi = x % 2, x // 2
    rep = hi * 2 + core
    me = lo * 16 + z * 4 + y
    other = 1 - core
    x_up, x_down, x_far = (x + 1) % 4, (x + 3) % 4, (x + 2) % 4
    up, down = device(x_up, y, z, core), device(x_down, y, z, core)
    partner = device(x, y, z, other)
    peers = [partner, device(x_far, y, z, core), device(x_far, y, z, other)]

    tables = [
        pltpu.make_async_copy(a, b, table_sem.at[i])
        for i, (a, b) in enumerate(((owner_hbm, owner_v), (layer_hbm, layer_v)))
    ]
    for copy in tables:
        copy.start()

    mine = pl.ds(pl.multiple_of(core * HALF, 128), HALF)
    rest = pl.ds(pl.multiple_of(other * HALF, 128), HALF)
    loads = []
    for dz in DZ:
        tz = (z + dz) % 4
        loads.append((weights_hbm.at[:, :, tz, :, :, mine], w.at[:, :, tz, :, :, mine]))
        loads.append((momentum_hbm.at[:, :, tz, :, :, mine], m.at[:, :, tz, :, :, mine]))
    loads += [
        (basis_hbm, bt),
        (delta_hbm, d),
        (weights_hbm.at[:, :, :, :, :, rest], w.at[:, :, :, :, :, rest]),
        (momentum_hbm.at[:, :, :, :, :, rest], m.at[:, :, :, :, :, rest]),
    ]
    copies = [pltpu.make_async_copy(a, b, load_sem.at[i]) for i, (a, b) in enumerate(loads)]
    for copy in copies:
        copy.start()

    barrier = pltpu.get_barrier_semaphore()
    targets = [up, down] + peers
    for dy, dz in FAR:
        for tx in (x, hi * 2 + 1 - lo):
            targets.append(device(tx, (y + dy) % 4, (z + dz) % 4, core))
    for to in targets:
        pl.semaphore_signal(barrier, inc=1, device_id=to, device_id_type=MESH)

    row = lax.broadcasted_iota(jnp.int32, (256, 1), 0)
    lane256 = lax.broadcasted_iota(jnp.int32, (1, 256), 1)
    lane128 = lax.broadcasted_iota(jnp.int32, (1, 128), 1)
    lane32 = lax.broadcasted_iota(jnp.int32, (1, BLOCKS), 1)
    blk_col = lax.broadcasted_iota(jnp.int32, (BLOCKS, 1), 0)
    for copy in tables:
        copy.wait()
    layer_row = layer_v[...]
    owner_row = owner_v[...]
    layer_col = jnp.sum(jnp.where(row // 8 == lane32, layer_row, 0), axis=1, keepdims=True)
    in_layer = (lane256 // RANK) == layer_col
    low = lane128 < RANK
    owner_col = jnp.sum(jnp.where(blk_col == lane32, owner_row, 0), axis=1, keepdims=True)
    same = owner_col == owner_row
    slot_col = owner_col * 2 + jnp.sum(
        jnp.where(same & (lane32 < blk_col), 1, 0), axis=1, keepdims=True
    )
    slots[...] = jnp.sum(jnp.where(blk_col == lane128, slot_col, 0), axis=0, keepdims=True)

    def q_rows(k):
        tz = (z + DZ[k]) % 4
        copies[2 * k].wait()
        copies[2 * k + 1].wait()
        for half in range(2):
            @pl.when(core == half)
            def _():
                cols = slice(half * HALF, (half + 1) * HALF)
                for s in range(2):
                    q[:, tz, :, s] = w[s, :, tz, :, :, cols] - (
                        outer_rate * momentum_decay * momentum_decay
                    ) * m[s, :, tz, :, :, cols]

    def direct_copy(i):
        dy, dz = FAR[i]
        ty, tz = (y + dy) % 4, (z + dz) % 4
        return send(
            q.at[lo, tz, ty], r.at[core, me], far_send, far_recv.at[i], device(x, ty, tz, core)
        )

    def onward_copy(i):
        dy, dz = NEAR[i]
        ty, tz = (y + dy) % 4, (z + dz) % 4
        return send(
            q.at[1 - lo, tz, ty, hi], relay.at[z * 4 + y], relay_send, relay_recv.at[i],
            device(x, ty, tz, core),
        )

    onward = [onward_copy(i) for i in range(15)]
    direct = [direct_copy(i) for i in range(15)]
    own_copy = pltpu.make_async_copy(q.at[lo, z, y], r.at[core, me], own_sem.at[0])
    own_swap = send(q.at[lo, z, y], r.at[core, me], swap_send, swap_recv.at[15], partner)
    side = [
        send(q.at[1 - lo, z, y, hi], r.at[core, me, hi], side_send, side_recv.at[k, 15], to)
        for k, to in enumerate((up, down))
    ]

    q_rows(0)
    q_rows(1)
    pl.semaphore_wait(barrier, len(targets))
    for copy in side + onward[:3]:
        copy.start()
    q_rows(2)
    for copy in onward[3:7]:
        copy.start()
    q_rows(3)
    for copy in onward[7:11]:
        copy.start()
    own_copy.start()
    own_swap.start()

    copies[8].wait()
    for t in range(D // TILE):
        cols = slice(t * TILE, (t + 1) * TILE)
        bt_high[:, cols], bt_low[:, cols] = split(bt[:, cols])
    for copy in onward[11:] + direct[:FIRST]:
        copy.start()
    copies[9].wait()
    every = jnp.zeros((256, 256), F32)
    for t in range(D // TILE):
        cols = slice(t * TILE, (t + 1) * TILE)
        high, low_part = split(d[:, cols])
        along = ((1,), (1,))
        every = every + (
            dot(high, bt_high[:, cols], along)
            + (dot(high, bt_low[:, cols], along) + dot(low_part, bt_high[:, cols], along))
        )
    every = jnp.where(in_layer, every, 0.0)
    both = every[:, :128] + every[:, 128:]
    both = both + pltpu.roll(both, RANK, 1)
    parts[rep] = jnp.where(low, both[:128], both[128:])

    layer_blk = jnp.sum(jnp.where(blk_col == lane32, layer_row, 0), axis=1, keepdims=True)
    slot_lane = jnp.sum(jnp.where(lane256 // 8 == blk_col, slot_col, 0), axis=0, keepdims=True)
    same_row = (row % 8) == (lane256 % 8)
    pick = [
        jnp.where(((row // 8) * 2 + j == slot_lane) & same_row, 1.0, 0.0) for j in range(2)
    ]
    used, layers = [], []
    for j in range(2):
        hit = slot_col == me * 2 + j
        used.append(jnp.sum(jnp.where(hit, 1.0, 0.0), axis=0, keepdims=True))
        layers.append(jnp.sum(jnp.where(hit, layer_blk, 0), axis=0, keepdims=True))

    part_copies = [
        send(parts.at[rep], parts.at[rep], part_send.at[k], part_recv.at[k], to)
        for k, to in enumerate(peers)
    ]
    for copy in part_copies[1:] + part_copies[:1]:
        copy.start()

    def source(dy, dz):
        return (y + 4 - dy) % 4, (z + 4 - dz) % 4

    def onward_step(i):
        fy, fz = source(*NEAR[i])
        src = lo * 16 + fz * 4 + fy
        onward[i].wait_recv()
        for k, to in enumerate((up, down)):
            send(relay.at[fz * 4 + fy], r.at[core, src, hi], side_send, side_recv.at[k, i], to).start()

    def swap_step(i):
        fy, fz = source(*FAR[i])
        src = lo * 16 + fz * 4 + fy
        direct[i].wait_recv()
        send(r.at[core, src], r.at[core, src], swap_send, swap_recv.at[i], partner).start()

    def side_step(i):
        fy, fz = source(*(NEAR[i] if i < 15 else (0, 0)))
        src = (1 - lo) * 16 + fz * 4 + fy
        for k, from_x in enumerate((x_down, x_up)):
            send(
                relay.at[0], r.at[core, src, from_x // 2], side_send, side_recv.at[k, i], up
            ).wait_recv()
        send(r.at[core, src], r.at[core, src], swap_send, swap_recv.at[16 + i], partner).start()

    for i in range(9):
        onward_step(i)
    for copy in part_copies:
        copy.wait_recv()
    averaged = ((parts[0] + parts[1]) + (parts[2] + parts[3])) * 0.25
    turned = pltpu.roll(averaged, RANK, 1)
    dup = jnp.concatenate(
        [jnp.where(low, averaged, turned), jnp.where(low, turned, averaged)], axis=0
    )
    chosen = [
        jnp.dot(p, dup, precision=HIGHEST, preferred_element_type=F32) for p in pick
    ]
    packed[...] = jnp.where(low, chosen[0], chosen[1]).reshape(OWN, 8, 128)

    def spread(pairs, keep):
        return jnp.where(keep, jnp.concatenate([pairs, pairs], axis=1), 0.0)

    og_high, og_low = split(spread(dup, in_layer))

    own_packed = pltpu.make_async_copy(packed.at[me], placed.at[me], own_sem.at[1])
    own_packed.start()
    for dy, dz in FAR + [(0, 0)]:
        for s in range(2):
            if s == 0 and (dy, dz) == (0, 0):
                continue
            ty, tz = (y + dy) % 4, (z + dz) % 4
            to_lo = lo if s == 0 else 1 - lo
            send(
                packed.at[to_lo * 16 + tz * 4 + ty], placed.at[me], packed_send,
                packed_recv, device(hi * 2 + to_lo, ty, tz, core),
            ).start()
    for copy in direct[FIRST:]:
        copy.start()

    for i in range(9, 15):
        onward_step(i)

    def og_body(t, carry):
        cols = pl.ds(pl.multiple_of(t * TILE, TILE), TILE)
        high = bt_high[:, cols]
        og[:, cols] = dot(og_high, high) + (dot(og_high, bt_low[:, cols]) + dot(og_low, high))
        return carry

    lax.fori_loop(0, D // TILE, og_body, 0)
    for i in (15, *range(7)):
        side_step(i)
    for i in range(FIRST):
        swap_step(i)

    own_packed.wait()
    tiles = send(packed.at[pl.ds(0, 31)], placed.at[pl.ds(0, 31)], packed_send, packed_recv, up)
    tiles.wait_recv()
    copies[10].wait()
    copies[11].wait()
    got = placed[...].reshape(256, 128)
    got_turned = pltpu.roll(got, RANK, 1)
    for j in range(2):
        pairs = jnp.where(low, got, got_turned) if j == 0 else jnp.where(low, got_turned, got)
        in_slot = jnp.broadcast_to((lane256 // RANK) == layers[j], (256, 256))
        slot_high, slot_low = split(spread(pairs, in_slot))
        use = used[j]

        def owner_body(t, carry, j=j, slot_high=slot_high, slot_low=slot_low, use=use):
            cols = pl.ds(pl.multiple_of(t * TILE, TILE), TILE)
            high = bt_high[:, cols]
            grad = dot(slot_high, high) + (dot(slot_high, bt_low[:, cols]) + dot(slot_low, high))
            moved = (momentum_decay * m[j, :, :, :, :, cols].reshape(256, TILE) + grad) * use
            new_momentum[j, :, cols] = moved
            new_weights[j, :, cols] = (
                w[j, :, :, :, :, cols].reshape(256, TILE)
                - outer_rate * (grad + momentum_decay * moved)
            ) * use
            return carry

        lax.fori_loop(0, D // TILE, owner_body, 0)
        if j == 0:
            for i in range(7, 15):
                side_step(i)

    for i in range(FIRST, 15):
        swap_step(i)
    own_copy.wait()
    for i in range(32):
        send(r.at[0, 0], r.at[other, 0], swap_send, swap_recv.at[i], partner).wait_recv()

    flat = r.at[0]
    send(flat.at[pl.ds(0, 15)], flat.at[pl.ds(0, 15)], far_send, far_recv.at[0], up).wait_send()
    send(relay.at[pl.ds(0, 15)], relay.at[pl.ds(0, 15)], relay_send, far_recv.at[0], up).wait_send()
    send(flat.at[pl.ds(0, 16)], flat.at[pl.ds(0, 16)], side_send, far_recv.at[0], up).wait_send()
    send(flat, flat, swap_send, far_recv.at[0], up).wait_send()
    tiles.wait_send()
    for copy in part_copies:
        copy.wait_send()


def finish(new_weights_v, new_momentum_v, r, og, slots_v, new_weights, new_momentum, replica,
           rows, slots, sem, slot_sem):
    slot_copy = pltpu.make_async_copy(slots_v, slots, slot_sem)
    slot_copy.start()
    pairs = []
    for a, b in ((new_weights_v, new_weights), (new_momentum_v, new_momentum)):
        pairs += [
            (a.at[s, pl.ds(h * 128, 128)], b.at[s, pl.ds(h * 128, 128)])
            for s in range(2) for h in range(2)
        ]
    pairs += [(rows.at[pl.ds(g * 8, 8)], replica.at[pl.ds(g * 8, 8)]) for g in range(4)]
    copies = [pltpu.make_async_copy(a, b, sem.at[i]) for i, (a, b) in enumerate(pairs)]
    for copy in copies[:8]:
        copy.start()
    slot_copy.wait()

    def out_body(b, carry):
        slot = slots[0, b]
        for half in range(2):
            cols = slice(half * HALF, (half + 1) * HALF)
            rows[b, :, cols] = r[half, slot // 2, slot % 2] - (
                outer_rate * (1.0 + momentum_decay)
            ) * og[pl.ds(pl.multiple_of(b * 8, 8), 8), cols]
        return carry

    for g in range(4):
        lax.fori_loop(g * 8, g * 8 + 8, out_body, 0)
        if g > 0:
            copies[8 + g - 1].start()
    copies[11].start()
    for copy in copies:
        copy.wait()


def local(replica_delta, layer_basis, layer_of, owner_of, weights_owned, momentum_owned):
    vmem = pl.BlockSpec(memory_space=pltpu.VMEM)
    hbm = pl.BlockSpec(memory_space=pltpu.HBM)
    dma = pltpu.SemaphoreType.DMA
    basis = jnp.swapaxes(layer_basis, 1, 2).reshape(4 * RANK, D)
    delta = replica_delta.reshape(256, D)
    weights = weights_owned.reshape(2, 2, 4, 4, 8, D)
    momentum = momentum_owned.reshape(2, 2, 4, 4, 8, D)
    between = pl.pallas_call(
        exchange,
        out_shape=(
            pltpu.VMEM((2, 256, D), F32),
            pltpu.VMEM((2, 256, D), F32),
            pltpu.VMEM((2, OWN, 2, 8, HALF), F32),
            pltpu.VMEM((256, D), F32),
            pltpu.VMEM((1, 128), jnp.int32),
        ),
        in_specs=[hbm] * 6,
        out_specs=(vmem,) * 5,
        scratch_shapes=[
            pltpu.VMEM((1, BLOCKS), jnp.int32),
            pltpu.VMEM((1, BLOCKS), jnp.int32),
            pltpu.VMEM((2, 2, 4, 4, 8, D), F32),
            pltpu.VMEM((2, 2, 4, 4, 8, D), F32),
            pltpu.VMEM((256, D), F32),
            pltpu.VMEM((256, D), F32),
            pltpu.VMEM((256, D), BF16),
            pltpu.VMEM((256, D), BF16),
            pltpu.VMEM((2, 4, 4, 2, 8, HALF), F32),
            pltpu.VMEM((16, 8, HALF), F32),
            pltpu.VMEM((4, 128, 128), F32),
            pltpu.VMEM((OWN, 8, 128), F32),
            pltpu.VMEM((OWN, 8, 128), F32),
            dma((12,)),
            dma, dma((15,)),
            dma, dma((15,)),
            dma, dma((2, 16)),
            dma, dma((32,)),
            dma((3,)), dma((3,)),
            dma, dma,
            dma((2,)),
            dma((2,)),
        ],
        compiler_params=pltpu.CompilerParams(
            collective_id=0, has_side_effects=True, vmem_limit_bytes=40 << 20
        ),
        name="outer_step",
    )(owner_of.reshape(1, BLOCKS), layer_of.reshape(1, BLOCKS), delta, basis, weights, momentum)
    shapes = ((2, 256, D), (2, 256, D), (BLOCKS, 8, D))
    return pl.pallas_call(
        finish,
        out_shape=tuple(jax.ShapeDtypeStruct(shape, F32) for shape in shapes),
        in_specs=[vmem] * 5,
        out_specs=(hbm,) * 3,
        scratch_shapes=[
            pltpu.VMEM((BLOCKS, 8, D), F32), pltpu.SMEM((1, 128), jnp.int32), dma((12,)), dma,
        ],
        compiler_params=pltpu.CompilerParams(vmem_limit_bytes=24 << 20),
        name="finish",
    )(*between)


def solution(mesh):
    placed = (
        P("rep", None, "own", None),
        P(),
        P(),
        P(),
        P("own", None, None),
        P("own", None, None),
    )
    return jax.shard_map(
        local,
        mesh=mesh,
        in_specs=placed,
        out_specs=(P("own", None, None), P("own", None, None), P(None, "own", None)),
        check_vma=False,
    )
```

```python
import jax
import jax.numpy as jnp
from jax import lax
from jax.experimental import pallas as pl
from jax.experimental.pallas import tpu as pltpu
from jax.sharding import PartitionSpec as P

momentum_decay = 0.9
outer_rate = 0.7

MESH = pl.DeviceIdType.MESH
HIGHEST = lax.Precision.HIGHEST
D = 1792
HALF = D // 2
RANK = 64
BLOCKS = 32
OWN = 32
TILE = 256
BF16 = jnp.bfloat16
F32 = jnp.float32

DZ = [0, 1, 3, 2]
NEAR = [(1, 0), (3, 0), (2, 0)] + [(dy, dz) for dz in DZ[1:] for dy in (0, 1, 3, 2)]
FAR = [(1, 2), (3, 2), (2, 1), (2, 3), (1, 1), (3, 3), (1, 3), (3, 1), (2, 2),
       (2, 0), (0, 2), (1, 0), (0, 1), (3, 0), (0, 3)]
FIRST = 10
PASSES = [("side", 15)] + [("side", i) for i in range(5)] + [("swap", i) for i in range(5)]
PASSES += [("side", i) for i in range(5, 10)] + [("swap", i) for i in range(5, 10)]
PASSES += [("side", i) for i in range(10, 15)] + [("swap", i) for i in range(10, 15)]


def place():
    rep = lax.axis_index("rep")
    own = lax.axis_index("own")
    x = (rep // 2) * 2 + own // 16
    return x, own % 4, (own // 4) % 4, rep % 2


def device(x, y, z, core):
    return ((x // 2) * 2 + core, (x % 2) * 16 + z * 4 + y)


def send(src, dst, send_sem, recv_sem, to):
    return pltpu.make_async_remote_copy(
        src_ref=src, dst_ref=dst, send_sem=send_sem, recv_sem=recv_sem,
        device_id=to, device_id_type=MESH,
    )


def split(value):
    high = value.astype(BF16)
    return high, (value - high.astype(F32)).astype(BF16)


def dot(a, b, dims=((1,), (0,))):
    return lax.dot_general(a, b, (dims, ((), ())), preferred_element_type=F32)


def exchange(
    owner_hbm, layer_hbm, delta_hbm, basis_hbm, weights_hbm, momentum_hbm,
    w, m, r, og, placed, terms, table,
    owner_v, layer_v, d, bt, q, relay, parts, packed,
    load_sem, far_send, far_recv, relay_send, relay_recv, side_send, side_recv,
    swap_send, swap_recv, part_send, part_recv, packed_send, packed_recv, own_sem,
    table_sem,
):
    x, y, z, core = place()
    lo, hi = x % 2, x // 2
    rep = hi * 2 + core
    me = lo * 16 + z * 4 + y
    other = 1 - core
    x_up, x_down, x_far = (x + 1) % 4, (x + 3) % 4, (x + 2) % 4
    up, down = device(x_up, y, z, core), device(x_down, y, z, core)
    partner = device(x, y, z, other)
    peers = [partner, device(x_far, y, z, core), device(x_far, y, z, other)]

    tables = [
        pltpu.make_async_copy(a, b, table_sem.at[i])
        for i, (a, b) in enumerate(((owner_hbm, owner_v), (layer_hbm, layer_v)))
    ]
    for copy in tables:
        copy.start()

    mine = pl.ds(pl.multiple_of(core * HALF, 128), HALF)
    rest = pl.ds(pl.multiple_of(other * HALF, 128), HALF)
    loads = []
    for dz in DZ:
        tz = (z + dz) % 4
        loads.append((weights_hbm.at[:, :, tz, :, :, mine], w.at[:, :, tz, :, :, mine]))
        loads.append((momentum_hbm.at[:, :, tz, :, :, mine], m.at[:, :, tz, :, :, mine]))
    loads += [
        (basis_hbm, bt),
        (delta_hbm, d),
        (weights_hbm.at[:, :, :, :, :, rest], w.at[:, :, :, :, :, rest]),
        (momentum_hbm.at[:, :, :, :, :, rest], m.at[:, :, :, :, :, rest]),
    ]
    copies = [pltpu.make_async_copy(a, b, load_sem.at[i]) for i, (a, b) in enumerate(loads)]
    for copy in copies:
        copy.start()

    barrier = pltpu.get_barrier_semaphore()
    targets = [up, down] + peers
    for dy, dz in FAR:
        for tx in (x, hi * 2 + 1 - lo):
            targets.append(device(tx, (y + dy) % 4, (z + dz) % 4, core))
    for to in targets:
        pl.semaphore_signal(barrier, inc=1, device_id=to, device_id_type=MESH)

    row = lax.broadcasted_iota(jnp.int32, (256, 1), 0)
    lane256 = lax.broadcasted_iota(jnp.int32, (1, 256), 1)
    lane128 = lax.broadcasted_iota(jnp.int32, (1, 128), 1)
    lane32 = lax.broadcasted_iota(jnp.int32, (1, BLOCKS), 1)
    blk_col = lax.broadcasted_iota(jnp.int32, (BLOCKS, 1), 0)
    for copy in tables:
        copy.wait()
    layer_row = layer_v[...]
    owner_row = owner_v[...]
    layer_col = jnp.sum(jnp.where(row // 8 == lane32, layer_row, 0), axis=1, keepdims=True)
    in_layer = (lane256 // RANK) == layer_col
    low = lane128 < RANK
    owner_col = jnp.sum(jnp.where(blk_col == lane32, owner_row, 0), axis=1, keepdims=True)
    same = owner_col == owner_row
    slot_col = owner_col * 2 + jnp.sum(
        jnp.where(same & (lane32 < blk_col), 1, 0), axis=1, keepdims=True
    )
    layer_blk = jnp.sum(jnp.where(blk_col == lane32, layer_row, 0), axis=1, keepdims=True)
    entry = jnp.where(blk_col == lane128, slot_col, 0)
    for j in range(2):
        hit = slot_col == me * 2 + j
        entry = entry + jnp.where(hit & (lane128 == 32 + j), layer_blk, 0)
        entry = entry + jnp.where(hit & (lane128 == 34 + j), 1, 0)
    table[...] = jnp.sum(entry, axis=0, keepdims=True)

    def q_rows(k):
        tz = (z + DZ[k]) % 4
        copies[2 * k].wait()
        copies[2 * k + 1].wait()
        for half in range(2):
            @pl.when(core == half)
            def _():
                cols = slice(half * HALF, (half + 1) * HALF)
                for s in range(2):
                    q[:, tz, :, s] = w[s, :, tz, :, :, cols] - (
                        outer_rate * momentum_decay * momentum_decay
                    ) * m[s, :, tz, :, :, cols]

    def direct_copy(i):
        dy, dz = FAR[i]
        ty, tz = (y + dy) % 4, (z + dz) % 4
        return send(
            q.at[lo, tz, ty], r.at[core, me], far_send, far_recv.at[i], device(x, ty, tz, core)
        )

    def onward_copy(i):
        dy, dz = NEAR[i]
        ty, tz = (y + dy) % 4, (z + dz) % 4
        return send(
            q.at[1 - lo, tz, ty, hi], relay.at[z * 4 + y], relay_send, relay_recv.at[i],
            device(x, ty, tz, core),
        )

    onward = [onward_copy(i) for i in range(15)]
    direct = [direct_copy(i) for i in range(15)]
    own_copy = pltpu.make_async_copy(q.at[lo, z, y], r.at[core, me], own_sem.at[0])
    own_swap = send(q.at[lo, z, y], r.at[core, me], swap_send, swap_recv.at[15], partner)
    side = [
        send(q.at[1 - lo, z, y, hi], r.at[core, me, hi], side_send, side_recv.at[k, 15], to)
        for k, to in enumerate((up, down))
    ]

    q_rows(0)
    q_rows(1)
    pl.semaphore_wait(barrier, len(targets))
    for copy in side + onward[:3]:
        copy.start()
    q_rows(2)
    for copy in onward[3:7]:
        copy.start()
    q_rows(3)
    for copy in onward[7:11]:
        copy.start()
    own_copy.start()
    own_swap.start()

    copies[8].wait()
    for t in range(D // TILE):
        cols = slice(t * TILE, (t + 1) * TILE)
        high, low_part = split(bt[:, :, cols])
        for k, term in enumerate((high, low_part, high, low_part)):
            terms[:, k * RANK:(k + 1) * RANK, cols] = term

    def basis_terms(cols):
        return [terms[:, k * RANK:(k + 1) * RANK, cols].reshape(256, TILE) for k in range(2)]

    for copy in onward[11:] + direct[:FIRST]:
        copy.start()
    copies[9].wait()
    every = jnp.zeros((256, 256), F32)
    for t in range(D // TILE):
        cols = slice(t * TILE, (t + 1) * TILE)
        high, low_part = split(d[:, cols])
        along = ((1,), (1,))
        bt_high, bt_low = basis_terms(cols)
        every = every + (
            dot(high, bt_high, along) + (dot(high, bt_low, along) + dot(low_part, bt_high, along))
        )
    every = jnp.where(in_layer, every, 0.0)
    both = every[:, :128] + every[:, 128:]
    both = both + pltpu.roll(both, RANK, 1)
    parts[rep] = jnp.where(low, both[:128], both[128:])

    slot_lane = jnp.sum(jnp.where(lane256 // 8 == blk_col, slot_col, 0), axis=0, keepdims=True)
    same_row = (row % 8) == (lane256 % 8)
    pick = [
        jnp.where(((row // 8) * 2 + j == slot_lane) & same_row, 1.0, 0.0) for j in range(2)
    ]

    part_copies = [
        send(parts.at[rep], parts.at[rep], part_send.at[k], part_recv.at[k], to)
        for k, to in enumerate(peers)
    ]
    for copy in part_copies[1:] + part_copies[:1]:
        copy.start()

    def source(dy, dz):
        return (y + 4 - dy) % 4, (z + 4 - dz) % 4

    def onward_step(i):
        fy, fz = source(*NEAR[i])
        src = lo * 16 + fz * 4 + fy
        onward[i].wait_recv()
        for k, to in enumerate((up, down)):
            send(relay.at[fz * 4 + fy], r.at[core, src, hi], side_send, side_recv.at[k, i], to).start()

    def swap_step(i):
        fy, fz = source(*FAR[i])
        src = lo * 16 + fz * 4 + fy
        direct[i].wait_recv()
        send(r.at[core, src], r.at[core, src], swap_send, swap_recv.at[i], partner).start()

    def side_step(i):
        fy, fz = source(*(NEAR[i] if i < 15 else (0, 0)))
        src = (1 - lo) * 16 + fz * 4 + fy
        for k, from_x in enumerate((x_down, x_up)):
            send(
                relay.at[0], r.at[core, src, from_x // 2], side_send, side_recv.at[k, i], up
            ).wait_recv()
        send(r.at[core, src], r.at[core, src], swap_send, swap_recv.at[16 + i], partner).start()

    for i in range(9):
        onward_step(i)
    for copy in part_copies:
        copy.wait_recv()
    averaged = ((parts[0] + parts[1]) + (parts[2] + parts[3])) * 0.25
    turned = pltpu.roll(averaged, RANK, 1)
    dup = jnp.concatenate(
        [jnp.where(low, averaged, turned), jnp.where(low, turned, averaged)], axis=0
    )
    chosen = [
        jnp.dot(p, dup, precision=HIGHEST, preferred_element_type=F32) for p in pick
    ]
    packed[...] = jnp.where(low, chosen[0], chosen[1]).reshape(OWN, 8, 128)

    def spread(pairs, keep):
        return jnp.where(keep, jnp.concatenate([pairs, pairs], axis=1), 0.0)

    og_high, og_low = split(spread(dup, in_layer))

    own_packed = pltpu.make_async_copy(packed.at[me], placed.at[me], own_sem.at[1])
    own_packed.start()
    for dy, dz in FAR + [(0, 0)]:
        for s in range(2):
            if s == 0 and (dy, dz) == (0, 0):
                continue
            ty, tz = (y + dy) % 4, (z + dz) % 4
            to_lo = lo if s == 0 else 1 - lo
            send(
                packed.at[to_lo * 16 + tz * 4 + ty], placed.at[me], packed_send,
                packed_recv, device(hi * 2 + to_lo, ty, tz, core),
            ).start()
    for copy in direct[FIRST:]:
        copy.start()

    for i in range(9, 15):
        onward_step(i)

    def og_body(t, carry):
        cols = pl.ds(pl.multiple_of(t * TILE, TILE), TILE)
        bt_high, bt_low = basis_terms(cols)
        og[:, cols] = dot(og_high, bt_high) + (dot(og_high, bt_low) + dot(og_low, bt_high))
        return carry

    lax.fori_loop(0, D // TILE, og_body, 0)
    for kind, i in PASSES:
        (side_step if kind == "side" else swap_step)(i)
    own_packed.wait()
    tiles = send(packed.at[pl.ds(0, 31)], placed.at[pl.ds(0, 31)], packed_send, packed_recv, up)
    tiles.wait_recv()
    copies[10].wait()
    copies[11].wait()
    own_copy.wait()
    for i in range(32):
        send(r.at[0, 0], r.at[other, 0], swap_send, swap_recv.at[i], partner).wait_recv()

    flat = r.at[0]
    send(flat.at[pl.ds(0, 15)], flat.at[pl.ds(0, 15)], far_send, far_recv.at[0], up).wait_send()
    send(relay.at[pl.ds(0, 15)], relay.at[pl.ds(0, 15)], relay_send, far_recv.at[0], up).wait_send()
    send(flat.at[pl.ds(0, 16)], flat.at[pl.ds(0, 16)], side_send, far_recv.at[0], up).wait_send()
    send(flat, flat, swap_send, far_recv.at[0], up).wait_send()
    tiles.wait_send()
    for copy in part_copies:
        copy.wait_send()


def finish(
    w, m, r, og, placed, terms, table_v, new_weights, new_momentum, replica,
    moved_w, moved_m, rows, table, sem, row_sem, table_sem,
):
    table_copy = pltpu.make_async_copy(table_v, table, table_sem)
    table_copy.start()
    got = placed[...].reshape(256, 128)
    got_turned = pltpu.roll(got, RANK, 1)
    low = lax.broadcasted_iota(jnp.int32, (1, 128), 1) < RANK
    sides = []
    for j in range(2):
        pairs = jnp.where(low, got, got_turned) if j == 0 else jnp.where(low, got_turned, got)
        sides.append(jnp.concatenate(split(pairs), axis=1))
    table_copy.wait()

    copies = []

    def issue(k):
        for copy in copies[2 * k:2 * k + 2]:
            copy.start()

    for j in range(2):
        layer = table[0, 32 + j]
        use = table[0, 34 + j].astype(F32)
        for t in range(D // TILE):
            cols = slice(t * TILE, (t + 1) * TILE)
            k = j * (D // TILE) + t
            grad = dot(sides[j], terms[layer, :, cols])
            moved = (momentum_decay * m[j, :, :, :, :, cols].reshape(256, TILE) + grad) * use
            moved_m[j, :, cols] = moved
            moved_w[j, :, cols] = (
                w[j, :, :, :, :, cols].reshape(256, TILE)
                - outer_rate * (grad + momentum_decay * moved)
            ) * use
            copies.append(pltpu.make_async_copy(
                moved_m.at[j, :, cols], new_momentum.at[j, :, cols], sem.at[0, k]))
            copies.append(pltpu.make_async_copy(
                moved_w.at[j, :, cols], new_weights.at[j, :, cols], sem.at[1, k]))
            if k > 0:
                issue(k - 1)

    def out_body(b, carry):
        slot = table[0, b]
        for half in range(2):
            cols = slice(half * HALF, (half + 1) * HALF)
            rows[b, :, cols] = r[half, slot // 2, slot % 2] - (
                outer_rate * (1.0 + momentum_decay)
            ) * og[pl.ds(pl.multiple_of(b * 8, 8), 8), cols]
        return carry

    row_copies = [
        pltpu.make_async_copy(rows.at[pl.ds(g * 8, 8)], replica.at[pl.ds(g * 8, 8)], row_sem.at[g])
        for g in range(4)
    ]
    for g in range(4):
        lax.fori_loop(g * 8, g * 8 + 8, out_body, 0)
        if g == 0:
            issue(2 * (D // TILE) - 1)
        else:
            row_copies[g - 1].start()
    row_copies[3].start()
    for copy in copies + row_copies:
        copy.wait()


def local(replica_delta, layer_basis, layer_of, owner_of, weights_owned, momentum_owned):
    vmem = pl.BlockSpec(memory_space=pltpu.VMEM)
    hbm = pl.BlockSpec(memory_space=pltpu.HBM)
    dma = pltpu.SemaphoreType.DMA
    basis = jnp.swapaxes(layer_basis, 1, 2)
    delta = replica_delta.reshape(256, D)
    weights = weights_owned.reshape(2, 2, 4, 4, 8, D)
    momentum = momentum_owned.reshape(2, 2, 4, 4, 8, D)
    between = pl.pallas_call(
        exchange,
        out_shape=(
            pltpu.VMEM((2, 2, 4, 4, 8, D), F32),
            pltpu.VMEM((2, 2, 4, 4, 8, D), F32),
            pltpu.VMEM((2, OWN, 2, 8, HALF), F32),
            pltpu.VMEM((256, D), F32),
            pltpu.VMEM((OWN, 8, 128), F32),
            pltpu.VMEM((4, 4 * RANK, D), BF16),
            pltpu.VMEM((1, 128), jnp.int32),
        ),
        in_specs=[hbm] * 6,
        out_specs=(vmem,) * 7,
        scratch_shapes=[
            pltpu.VMEM((1, BLOCKS), jnp.int32),
            pltpu.VMEM((1, BLOCKS), jnp.int32),
            pltpu.VMEM((256, D), F32),
            pltpu.VMEM((4, RANK, D), F32),
            pltpu.VMEM((2, 4, 4, 2, 8, HALF), F32),
            pltpu.VMEM((16, 8, HALF), F32),
            pltpu.VMEM((4, 128, 128), F32),
            pltpu.VMEM((OWN, 8, 128), F32),
            dma((12,)),
            dma, dma((15,)),
            dma, dma((15,)),
            dma, dma((2, 16)),
            dma, dma((32,)),
            dma((3,)), dma((3,)),
            dma, dma,
            dma((2,)),
            dma((2,)),
        ],
        compiler_params=pltpu.CompilerParams(
            collective_id=0, has_side_effects=True, vmem_limit_bytes=45 << 20
        ),
        name="outer_step",
    )(owner_of.reshape(1, BLOCKS), layer_of.reshape(1, BLOCKS), delta, basis, weights, momentum)
    shapes = ((2, 256, D), (2, 256, D), (BLOCKS, 8, D))
    return pl.pallas_call(
        finish,
        out_shape=tuple(jax.ShapeDtypeStruct(shape, F32) for shape in shapes),
        in_specs=[vmem] * 7,
        out_specs=(hbm,) * 3,
        scratch_shapes=[
            pltpu.VMEM((2, 256, D), F32), pltpu.VMEM((2, 256, D), F32),
            pltpu.VMEM((BLOCKS, 8, D), F32), pltpu.SMEM((1, 128), jnp.int32),
            dma((2, 14)), dma((4,)), dma,
        ],
        compiler_params=pltpu.CompilerParams(vmem_limit_bytes=16 << 20),
        name="finish",
    )(*between)


def solution(mesh):
    placed = (
        P("rep", None, "own", None),
        P(),
        P(),
        P(),
        P("own", None, None),
        P("own", None, None),
    )
    return jax.shard_map(
        local,
        mesh=mesh,
        in_specs=placed,
        out_specs=(P("own", None, None), P("own", None, None), P(None, "own", None)),
        check_vma=False,
    )
```

```python
import jax
import jax.numpy as jnp
from jax import lax
from jax.experimental import pallas as pl
from jax.experimental.pallas import tpu as pltpu
from jax.sharding import PartitionSpec as P

momentum_decay = 0.9
outer_rate = 0.7

MESH = pl.DeviceIdType.MESH
HIGHEST = lax.Precision.HIGHEST
D = 1792
HALF = D // 2
RANK = 64
BLOCKS = 32
OWN = 32
TILE = 256
BF16 = jnp.bfloat16
F32 = jnp.float32

DZ = [0, 1, 3, 2]
NEAR = [(1, 0), (3, 0), (0, 1), (0, 3),
        (2, 0), (1, 1), (3, 3), (3, 1), (1, 3), (0, 2),
        (1, 2), (3, 2), (2, 1), (2, 3), (2, 2)]
FAR = [(1, 0), (3, 0), (0, 1), (0, 3),
       (2, 2), (1, 2), (3, 2), (2, 1), (2, 3),
       (1, 1), (3, 3), (3, 1), (1, 3), (2, 0), (0, 2)]
FIRST = 9
PASSES = [("swap", i) for i in range(4)] + [("side", 15)] + [("side", i) for i in range(4)]
PASSES += [("side", i) for i in range(4, 8)]
PASSES += [("swap", i) for i in range(4, 9)] + [("side", i) for i in range(8, 12)]
PASSES += [("swap", i) for i in range(9, 12)]
PASSES += [("side", i) for i in range(12, 15)] + [("swap", i) for i in range(12, 15)]


def place():
    rep = lax.axis_index("rep")
    own = lax.axis_index("own")
    x = (rep // 2) * 2 + own // 16
    return x, own % 4, (own // 4) % 4, rep % 2


def device(x, y, z, core):
    return ((x // 2) * 2 + core, (x % 2) * 16 + z * 4 + y)


def send(src, dst, send_sem, recv_sem, to):
    return pltpu.make_async_remote_copy(
        src_ref=src, dst_ref=dst, send_sem=send_sem, recv_sem=recv_sem,
        device_id=to, device_id_type=MESH,
    )


def split(value):
    high = value.astype(BF16)
    return high, (value - high.astype(F32)).astype(BF16)


def dot(a, b, dims=((1,), (0,))):
    return lax.dot_general(a, b, (dims, ((), ())), preferred_element_type=F32)


def exchange(
    owner_hbm, layer_hbm, delta_hbm, basis_hbm, weights_hbm, momentum_hbm,
    w, m, r, og, placed, terms, table,
    owner_v, layer_v, d, bt, q, relay, parts, packed,
    load_sem, far_send, far_recv, relay_send, relay_recv, side_send, side_recv,
    swap_send, swap_recv, part_send, part_recv, packed_send, packed_recv, own_sem,
    table_sem,
):
    x, y, z, core = place()
    lo, hi = x % 2, x // 2
    rep = hi * 2 + core
    me = lo * 16 + z * 4 + y
    other = 1 - core
    x_up, x_down, x_far = (x + 1) % 4, (x + 3) % 4, (x + 2) % 4
    up, down = device(x_up, y, z, core), device(x_down, y, z, core)
    partner = device(x, y, z, other)
    peers = [partner, device(x_far, y, z, core), device(x_far, y, z, other)]

    barrier = pltpu.get_barrier_semaphore()
    targets = []
    for dy, dz in reversed(NEAR):
        for tx in (hi * 2 + 1 - lo, x):
            targets.append(device(tx, (y + dy) % 4, (z + dz) % 4, core))
    targets += peers + [up, down]
    for to in targets:
        pl.semaphore_signal(barrier, inc=1, device_id=to, device_id_type=MESH)

    tables = [
        pltpu.make_async_copy(a, b, table_sem.at[i])
        for i, (a, b) in enumerate(((owner_hbm, owner_v), (layer_hbm, layer_v)))
    ]
    for copy in tables:
        copy.start()

    mine = pl.ds(pl.multiple_of(core * HALF, 128), HALF)
    rest = pl.ds(pl.multiple_of(other * HALF, 128), HALF)
    loads = []
    for dz in DZ:
        tz = (z + dz) % 4
        loads.append((weights_hbm.at[:, :, tz, :, :, mine], w.at[:, :, tz, :, :, mine]))
        loads.append((momentum_hbm.at[:, :, tz, :, :, mine], m.at[:, :, tz, :, :, mine]))
    loads += [
        (basis_hbm, bt),
        (delta_hbm, d),
        (weights_hbm.at[:, :, :, :, :, rest], w.at[:, :, :, :, :, rest]),
        (momentum_hbm.at[:, :, :, :, :, rest], m.at[:, :, :, :, :, rest]),
    ]
    copies = [pltpu.make_async_copy(a, b, load_sem.at[i]) for i, (a, b) in enumerate(loads)]
    for copy in copies:
        copy.start()

    def q_rows(k):
        tz = (z + DZ[k]) % 4
        copies[2 * k].wait()
        copies[2 * k + 1].wait()
        for half in range(2):
            @pl.when(core == half)
            def _():
                cols = slice(half * HALF, (half + 1) * HALF)
                for s in range(2):
                    q[:, tz, :, s] = w[s, :, tz, :, :, cols] - (
                        outer_rate * momentum_decay * momentum_decay
                    ) * m[s, :, tz, :, :, cols]

    def direct_copy(i):
        dy, dz = FAR[i]
        ty, tz = (y + dy) % 4, (z + dz) % 4
        return send(
            q.at[lo, tz, ty], r.at[core, me], far_send, far_recv.at[i], device(x, ty, tz, core)
        )

    def onward_copy(i):
        dy, dz = NEAR[i]
        ty, tz = (y + dy) % 4, (z + dz) % 4
        return send(
            q.at[1 - lo, tz, ty, hi], relay.at[z * 4 + y], relay_send, relay_recv.at[i],
            device(x, ty, tz, core),
        )

    onward = [onward_copy(i) for i in range(15)]
    direct = [direct_copy(i) for i in range(15)]
    own_copy = pltpu.make_async_copy(q.at[lo, z, y], r.at[core, me], own_sem.at[0])
    own_swap = send(q.at[lo, z, y], r.at[core, me], swap_send, swap_recv.at[15], partner)
    side = [
        send(q.at[1 - lo, z, y, hi], r.at[core, me, hi], side_send, side_recv.at[k, 15], to)
        for k, to in enumerate((up, down))
    ]

    q_rows(0)
    q_rows(1)
    pl.semaphore_wait(barrier, len(targets))
    for copy in side + onward[:2] + direct[:2]:
        copy.start()
    q_rows(2)
    for copy in (onward[2], direct[2]):
        copy.start()
    q_rows(3)
    for copy in (onward[3], direct[3]):
        copy.start()
    for copy in onward[4:10]:
        copy.start()
    for copy in onward[10:14]:
        copy.start()
    own_copy.start()
    own_swap.start()

    def source(dy, dz):
        return (y + 4 - dy) % 4, (z + 4 - dz) % 4

    def onward_step(i):
        fy, fz = source(*NEAR[i])
        src = lo * 16 + fz * 4 + fy
        onward[i].wait_recv()
        for k, to in enumerate((up, down)):
            send(relay.at[fz * 4 + fy], r.at[core, src, hi], side_send, side_recv.at[k, i], to).start()

    def swap_step(i):
        fy, fz = source(*FAR[i])
        src = lo * 16 + fz * 4 + fy
        direct[i].wait_recv()
        send(r.at[core, src], r.at[core, src], swap_send, swap_recv.at[i], partner).start()

    def side_step(i):
        fy, fz = source(*(NEAR[i] if i < 15 else (0, 0)))
        src = (1 - lo) * 16 + fz * 4 + fy
        for k, from_x in enumerate((x_down, x_up)):
            send(
                relay.at[0], r.at[core, src, from_x // 2], side_send, side_recv.at[k, i], up
            ).wait_recv()
        send(r.at[core, src], r.at[core, src], swap_send, swap_recv.at[16 + i], partner).start()

    row = lax.broadcasted_iota(jnp.int32, (256, 1), 0)
    lane256 = lax.broadcasted_iota(jnp.int32, (1, 256), 1)
    lane128 = lax.broadcasted_iota(jnp.int32, (1, 128), 1)
    lane32 = lax.broadcasted_iota(jnp.int32, (1, BLOCKS), 1)
    blk_col = lax.broadcasted_iota(jnp.int32, (BLOCKS, 1), 0)
    for copy in tables:
        copy.wait()
    layer_row = layer_v[...]
    owner_row = owner_v[...]
    layer_col = jnp.sum(jnp.where(row // 8 == lane32, layer_row, 0), axis=1, keepdims=True)
    in_layer = (lane256 // RANK) == layer_col
    low = lane128 < RANK
    owner_col = jnp.sum(jnp.where(blk_col == lane32, owner_row, 0), axis=1, keepdims=True)
    same = owner_col == owner_row
    slot_col = owner_col * 2 + jnp.sum(
        jnp.where(same & (lane32 < blk_col), 1, 0), axis=1, keepdims=True
    )
    layer_blk = jnp.sum(jnp.where(blk_col == lane32, layer_row, 0), axis=1, keepdims=True)
    entry = jnp.where(blk_col == lane128, slot_col, 0)
    for j in range(2):
        hit = slot_col == me * 2 + j
        entry = entry + jnp.where(hit & (lane128 == 32 + j), layer_blk, 0)
        entry = entry + jnp.where(hit & (lane128 == 34 + j), 1, 0)
    table[...] = jnp.sum(entry, axis=0, keepdims=True)

    copies[8].wait()
    for t in range(D // TILE):
        cols = slice(t * TILE, (t + 1) * TILE)
        high, low_part = split(bt[:, :, cols])
        for k, term in enumerate((high, low_part, high, low_part)):
            terms[:, k * RANK:(k + 1) * RANK, cols] = term

    def basis_terms(cols):
        return [terms[:, k * RANK:(k + 1) * RANK, cols].reshape(256, TILE) for k in range(2)]

    for copy in onward[14:] + direct[4:FIRST]:
        copy.start()
    copies[9].wait()
    every = jnp.zeros((256, 256), F32)
    for t in range(D // TILE):
        cols = slice(t * TILE, (t + 1) * TILE)
        high, low_part = split(d[:, cols])
        along = ((1,), (1,))
        bt_high, bt_low = basis_terms(cols)
        every = every + (
            dot(high, bt_high, along) + (dot(high, bt_low, along) + dot(low_part, bt_high, along))
        )
    every = jnp.where(in_layer, every, 0.0)
    both = every[:, :128] + every[:, 128:]
    both = both + pltpu.roll(both, RANK, 1)
    parts[rep] = jnp.where(low, both[:128], both[128:])

    slot_lane = jnp.sum(jnp.where(lane256 // 8 == blk_col, slot_col, 0), axis=0, keepdims=True)
    same_row = (row % 8) == (lane256 % 8)
    pick = [
        jnp.where(((row // 8) * 2 + j == slot_lane) & same_row, 1.0, 0.0) for j in range(2)
    ]

    part_copies = [
        send(parts.at[rep], parts.at[rep], part_send.at[k], part_recv.at[k], to)
        for k, to in enumerate(peers)
    ]
    for copy in part_copies[1:] + part_copies[:1]:
        copy.start()

    for i in range(9):
        onward_step(i)
    for copy in part_copies:
        copy.wait_recv()
    averaged = ((parts[0] + parts[1]) + (parts[2] + parts[3])) * 0.25
    turned = pltpu.roll(averaged, RANK, 1)
    dup = jnp.concatenate(
        [jnp.where(low, averaged, turned), jnp.where(low, turned, averaged)], axis=0
    )
    chosen = [
        jnp.dot(p, dup, precision=HIGHEST, preferred_element_type=F32) for p in pick
    ]
    packed[...] = jnp.where(low, chosen[0], chosen[1]).reshape(OWN, 8, 128)

    def spread(pairs, keep):
        return jnp.where(keep, jnp.concatenate([pairs, pairs], axis=1), 0.0)

    og_high, og_low = split(spread(dup, in_layer))

    takes = core == (lo + y + z + 1) % 2

    def send_tiles(parity):
        for dy, dz in NEAR[::-1] + [(0, 0)]:
            for s in range(2):
                if (dy + dz + s) % 2 != parity or (s == 0 and (dy, dz) == (0, 0)):
                    continue
                ty, tz = (y + dy) % 4, (z + dz) % 4
                to_lo = lo if s == 0 else 1 - lo
                send(
                    packed.at[to_lo * 16 + tz * 4 + ty], placed.at[me], packed_send.at[0],
                    packed_recv.at[0], device(hi * 2 + to_lo, ty, tz, core),
                ).start()

    own_packed = pltpu.make_async_copy(packed.at[me], placed.at[me], own_sem.at[1])

    @pl.when(takes)
    def _():
        own_packed.start()
        send_tiles(0)

    @pl.when(jnp.logical_not(takes))
    def _():
        send_tiles(1)

    for copy in direct[FIRST:]:
        copy.start()

    for i in range(9, 15):
        onward_step(i)

    def og_body(t, carry):
        cols = pl.ds(pl.multiple_of(t * TILE, TILE), TILE)
        bt_high, bt_low = basis_terms(cols)
        og[:, cols] = dot(og_high, bt_high) + (dot(og_high, bt_low) + dot(og_low, bt_high))
        return carry

    lax.fori_loop(0, D // TILE, og_body, 0)
    steps = {"side": side_step, "swap": swap_step}
    hand_over = send(placed, placed, packed_send.at[1], packed_recv.at[1], partner)
    tiles = [
        send(packed.at[pl.ds(0, n)], placed.at[pl.ds(0, n)], packed_send.at[0], packed_recv.at[0], up)
        for n in (15, 16, 31)
    ]
    late = 9
    for kind, i in PASSES[:-late]:
        steps[kind](i)

    @pl.when(takes)
    def _():
        own_packed.wait()
        tiles[2].wait_recv()
        hand_over.start()

    for kind, i in PASSES[-late:]:
        steps[kind](i)

    @pl.when(jnp.logical_not(takes))
    def _():
        hand_over.wait_recv()

    copies[10].wait()
    copies[11].wait()
    own_copy.wait()
    for i in range(32):
        send(r.at[0, 0], r.at[other, 0], swap_send, swap_recv.at[i], partner).wait_recv()

    flat = r.at[0]
    send(flat.at[pl.ds(0, 15)], flat.at[pl.ds(0, 15)], far_send, far_recv.at[0], up).wait_send()
    send(relay.at[pl.ds(0, 15)], relay.at[pl.ds(0, 15)], relay_send, far_recv.at[0], up).wait_send()
    send(flat.at[pl.ds(0, 16)], flat.at[pl.ds(0, 16)], side_send, far_recv.at[0], up).wait_send()
    send(flat, flat, swap_send, far_recv.at[0], up).wait_send()
    for copy in part_copies:
        copy.wait_send()

    @pl.when(takes)
    def _():
        tiles[0].wait_send()
        hand_over.wait_send()

    @pl.when(jnp.logical_not(takes))
    def _():
        tiles[1].wait_send()


def finish(
    w, m, r, og, placed, terms, table_v, new_weights, new_momentum, replica,
    moved_w, moved_m, rows, table, sem, row_sem, table_sem,
):
    table_copy = pltpu.make_async_copy(table_v, table, table_sem)
    table_copy.start()
    got = placed[...].reshape(256, 128)
    got_turned = pltpu.roll(got, RANK, 1)
    lane = lax.broadcasted_iota(jnp.int32, (1, 128), 1)
    low = lane < RANK
    sides = []
    for j in range(2):
        pairs = jnp.where(low, got, got_turned) if j == 0 else jnp.where(low, got_turned, got)
        sides.append(jnp.concatenate(split(pairs), axis=1))

    copies = []

    def issue(k):
        for copy in copies[2 * k:2 * k + 2]:
            copy.start()

    for j in range(2):
        layer = jnp.sum(jnp.where(lane == 32 + j, table_v[...], 0))
        use = jnp.where(lane == 34 + j, table_v[...], 0)
        use = jnp.sum(use, axis=1, keepdims=True).astype(F32)
        for t in range(D // TILE):
            cols = slice(t * TILE, (t + 1) * TILE)
            k = j * (D // TILE) + t
            grad = dot(sides[j], terms[layer, :, cols])
            moved = (momentum_decay * m[j, :, :, :, :, cols].reshape(256, TILE) + grad) * use
            moved_m[j, :, cols] = moved
            moved_w[j, :, cols] = (
                w[j, :, :, :, :, cols].reshape(256, TILE)
                - outer_rate * (grad + momentum_decay * moved)
            ) * use
            copies.append(pltpu.make_async_copy(
                moved_m.at[j, :, cols], new_momentum.at[j, :, cols], sem.at[0, k]))
            copies.append(pltpu.make_async_copy(
                moved_w.at[j, :, cols], new_weights.at[j, :, cols], sem.at[1, k]))
            if k > 0:
                issue(k - 1)

    def out_body(b, carry):
        slot = table[0, b]
        for half in range(2):
            cols = slice(half * HALF, (half + 1) * HALF)
            rows[b, :, cols] = r[half, slot // 2, slot % 2] - (
                outer_rate * (1.0 + momentum_decay)
            ) * og[pl.ds(pl.multiple_of(b * 8, 8), 8), cols]
        return carry

    row_copies = [
        pltpu.make_async_copy(rows.at[pl.ds(g * 8, 8)], replica.at[pl.ds(g * 8, 8)], row_sem.at[g])
        for g in range(4)
    ]
    table_copy.wait()
    for g in range(4):
        lax.fori_loop(g * 8, g * 8 + 8, out_body, 0)
        if g == 0:
            issue(2 * (D // TILE) - 1)
        else:
            row_copies[g - 1].start()
    row_copies[3].start()
    for copy in copies + row_copies:
        copy.wait()


def local(replica_delta, layer_basis, layer_of, owner_of, weights_owned, momentum_owned):
    vmem = pl.BlockSpec(memory_space=pltpu.VMEM)
    hbm = pl.BlockSpec(memory_space=pltpu.HBM)
    dma = pltpu.SemaphoreType.DMA
    basis = jnp.swapaxes(layer_basis, 1, 2)
    delta = replica_delta.reshape(256, D)
    weights = weights_owned.reshape(2, 2, 4, 4, 8, D)
    momentum = momentum_owned.reshape(2, 2, 4, 4, 8, D)
    between = pl.pallas_call(
        exchange,
        out_shape=(
            pltpu.VMEM((2, 2, 4, 4, 8, D), F32),
            pltpu.VMEM((2, 2, 4, 4, 8, D), F32),
            pltpu.VMEM((2, OWN, 2, 8, HALF), F32),
            pltpu.VMEM((256, D), F32),
            pltpu.VMEM((OWN, 8, 128), F32),
            pltpu.VMEM((4, 4 * RANK, D), BF16),
            pltpu.VMEM((1, 128), jnp.int32),
        ),
        in_specs=[hbm] * 6,
        out_specs=(vmem,) * 7,
        scratch_shapes=[
            pltpu.VMEM((1, BLOCKS), jnp.int32),
            pltpu.VMEM((1, BLOCKS), jnp.int32),
            pltpu.VMEM((256, D), F32),
            pltpu.VMEM((4, RANK, D), F32),
            pltpu.VMEM((2, 4, 4, 2, 8, HALF), F32),
            pltpu.VMEM((16, 8, HALF), F32),
            pltpu.VMEM((4, 128, 128), F32),
            pltpu.VMEM((OWN, 8, 128), F32),
            dma((12,)),
            dma, dma((15,)),
            dma, dma((15,)),
            dma, dma((2, 16)),
            dma, dma((32,)),
            dma((3,)), dma((3,)),
            dma((2,)), dma((2,)),
            dma((2,)),
            dma((2,)),
        ],
        compiler_params=pltpu.CompilerParams(
            collective_id=0, has_side_effects=True, vmem_limit_bytes=45 << 20
        ),
        name="outer_step",
    )(owner_of.reshape(1, BLOCKS), layer_of.reshape(1, BLOCKS), delta, basis, weights, momentum)
    shapes = ((2, 256, D), (2, 256, D), (BLOCKS, 8, D))
    return pl.pallas_call(
        finish,
        out_shape=tuple(jax.ShapeDtypeStruct(shape, F32) for shape in shapes),
        in_specs=[vmem] * 7,
        out_specs=(hbm,) * 3,
        scratch_shapes=[
            pltpu.VMEM((2, 256, D), F32), pltpu.VMEM((2, 256, D), F32),
            pltpu.VMEM((BLOCKS, 8, D), F32), pltpu.SMEM((1, 128), jnp.int32),
            dma((2, 14)), dma((4,)), dma,
        ],
        compiler_params=pltpu.CompilerParams(vmem_limit_bytes=16 << 20),
        name="finish",
    )(*between)


def solution(mesh):
    placed = (
        P("rep", None, "own", None),
        P(),
        P(),
        P(),
        P("own", None, None),
        P("own", None, None),
    )
    return jax.shard_map(
        local,
        mesh=mesh,
        in_specs=placed,
        out_specs=(P("own", None, None), P("own", None, None), P(None, "own", None)),
        check_vma=False,
    )
```

```python
import jax
import jax.numpy as jnp
from jax import lax
from jax.experimental import pallas as pl
from jax.experimental.pallas import tpu as pltpu
from jax.sharding import PartitionSpec as P

momentum_decay = 0.9
outer_rate = 0.7

MESH = pl.DeviceIdType.MESH
HIGHEST = lax.Precision.HIGHEST
D = 1792
HALF = D // 2
RANK = 64
BLOCKS = 32
OWN = 32
TILE = 256
BF16 = jnp.bfloat16
F32 = jnp.float32

DZ = [0, 1, 3, 2]
NEAR = [(1, 0), (3, 0), (0, 1), (0, 3),
        (2, 0), (1, 1), (3, 3), (3, 1), (1, 3), (0, 2),
        (1, 2), (3, 2), (2, 1), (2, 3), (2, 2)]
FAR = [(1, 0), (3, 0), (0, 1), (0, 3),
       (2, 2), (1, 2), (3, 2), (2, 1), (2, 3),
       (1, 1), (3, 3), (3, 1), (1, 3), (2, 0), (0, 2)]
FIRST = 9
PASSES = [("swap", i) for i in range(4)] + [("side", 15)] + [("side", i) for i in range(4)]
PASSES += [("side", i) for i in range(4, 8)]
PASSES += [("swap", i) for i in range(4, 9)] + [("side", i) for i in range(8, 12)]
PASSES += [("swap", i) for i in range(9, 12)]
PASSES += [("side", i) for i in range(12, 15)] + [("swap", i) for i in range(12, 15)]


def place():
    rep = lax.axis_index("rep")
    own = lax.axis_index("own")
    x = (rep // 2) * 2 + own // 16
    return x, own % 4, (own // 4) % 4, rep % 2


def device(x, y, z, core):
    return ((x // 2) * 2 + core, (x % 2) * 16 + z * 4 + y)


def send(src, dst, send_sem, recv_sem, to):
    return pltpu.make_async_remote_copy(
        src_ref=src, dst_ref=dst, send_sem=send_sem, recv_sem=recv_sem,
        device_id=to, device_id_type=MESH,
    )


def split(value):
    high = value.astype(BF16)
    return high, (value - high.astype(F32)).astype(BF16)


def dot(a, b, dims=((1,), (0,))):
    return lax.dot_general(a, b, (dims, ((), ())), preferred_element_type=F32)


def exchange(
    owner_hbm, layer_hbm, delta_hbm, basis_hbm, weights_hbm, momentum_hbm,
    w, m, r, og, placed, terms, table,
    owner_v, layer_v, d, bt, q, relay, parts, packed,
    load_sem, far_send, far_recv, relay_send, relay_recv, side_send, side_recv,
    swap_send, swap_recv, part_send, part_recv, packed_send, packed_recv, own_sem,
    table_sem,
):
    x, y, z, core = place()
    lo, hi = x % 2, x // 2
    rep = hi * 2 + core
    me = lo * 16 + z * 4 + y
    other = 1 - core
    x_up, x_down, x_far = (x + 1) % 4, (x + 3) % 4, (x + 2) % 4
    up, down = device(x_up, y, z, core), device(x_down, y, z, core)
    partner = device(x, y, z, other)
    peers = [partner, device(x_far, y, z, core), device(x_far, y, z, other)]

    barrier = pltpu.get_barrier_semaphore()
    targets = []
    for dy, dz in reversed(NEAR):
        for tx in (hi * 2 + 1 - lo, x):
            targets.append(device(tx, (y + dy) % 4, (z + dz) % 4, core))
    targets += peers + [up, down]
    for to in targets:
        pl.semaphore_signal(barrier, inc=1, device_id=to, device_id_type=MESH)

    tables = [
        pltpu.make_async_copy(a, b, table_sem.at[i])
        for i, (a, b) in enumerate(((owner_hbm, owner_v), (layer_hbm, layer_v)))
    ]
    for copy in tables:
        copy.start()

    mine = pl.ds(pl.multiple_of(core * HALF, 128), HALF)
    rest = pl.ds(pl.multiple_of(other * HALF, 128), HALF)
    loads = []
    for dz in DZ:
        tz = (z + dz) % 4
        loads.append((weights_hbm.at[:, :, tz, :, :, mine], w.at[:, :, tz, :, :, mine]))
        loads.append((momentum_hbm.at[:, :, tz, :, :, mine], m.at[:, :, tz, :, :, mine]))
    loads += [
        (basis_hbm, bt),
        (delta_hbm, d),
        (weights_hbm.at[:, :, :, :, :, rest], w.at[:, :, :, :, :, rest]),
        (momentum_hbm.at[:, :, :, :, :, rest], m.at[:, :, :, :, :, rest]),
    ]
    copies = [pltpu.make_async_copy(a, b, load_sem.at[i]) for i, (a, b) in enumerate(loads)]
    for copy in copies:
        copy.start()

    def q_rows(k):
        tz = (z + DZ[k]) % 4
        copies[2 * k].wait()
        copies[2 * k + 1].wait()
        for half in range(2):
            @pl.when(core == half)
            def _():
                cols = slice(half * HALF, (half + 1) * HALF)
                for s in range(2):
                    q[:, tz, :, s] = w[s, :, tz, :, :, cols] - (
                        outer_rate * momentum_decay * momentum_decay
                    ) * m[s, :, tz, :, :, cols]

    def direct_copy(i):
        dy, dz = FAR[i]
        ty, tz = (y + dy) % 4, (z + dz) % 4
        return send(
            q.at[lo, tz, ty], r.at[core, me], far_send, far_recv.at[i], device(x, ty, tz, core)
        )

    def onward_copy(i):
        dy, dz = NEAR[i]
        ty, tz = (y + dy) % 4, (z + dz) % 4
        return send(
            q.at[1 - lo, tz, ty, hi], relay.at[z * 4 + y], relay_send, relay_recv.at[i],
            device(x, ty, tz, core),
        )

    onward = [onward_copy(i) for i in range(15)]
    direct = [direct_copy(i) for i in range(15)]
    own_copy = pltpu.make_async_copy(q.at[lo, z, y], r.at[core, me], own_sem.at[0])
    own_swap = send(q.at[lo, z, y], r.at[core, me], swap_send, swap_recv.at[15], partner)
    side = [
        send(q.at[1 - lo, z, y, hi], r.at[core, me, hi], side_send, side_recv.at[k, 15], to)
        for k, to in enumerate((up, down))
    ]

    q_rows(0)
    q_rows(1)
    pl.semaphore_wait(barrier, len(targets))
    for copy in side + onward[:2]:
        copy.start()
    q_rows(2)
    onward[2].start()
    q_rows(3)
    for copy in onward[3:14]:
        copy.start()
    own_copy.start()
    own_swap.start()

    def source(dy, dz):
        return (y + 4 - dy) % 4, (z + 4 - dz) % 4

    def onward_step(i):
        fy, fz = source(*NEAR[i])
        src = lo * 16 + fz * 4 + fy
        onward[i].wait_recv()
        for k, to in enumerate((up, down)):
            send(relay.at[fz * 4 + fy], r.at[core, src, hi], side_send, side_recv.at[k, i], to).start()

    def swap_step(i):
        fy, fz = source(*FAR[i])
        src = lo * 16 + fz * 4 + fy
        direct[i].wait_recv()
        send(r.at[core, src], r.at[core, src], swap_send, swap_recv.at[i], partner).start()

    def side_step(i):
        fy, fz = source(*(NEAR[i] if i < 15 else (0, 0)))
        src = (1 - lo) * 16 + fz * 4 + fy
        for k, from_x in enumerate((x_down, x_up)):
            send(
                relay.at[0], r.at[core, src, from_x // 2], side_send, side_recv.at[k, i], up
            ).wait_recv()
        send(r.at[core, src], r.at[core, src], swap_send, swap_recv.at[16 + i], partner).start()

    row = lax.broadcasted_iota(jnp.int32, (256, 1), 0)
    lane256 = lax.broadcasted_iota(jnp.int32, (1, 256), 1)
    lane128 = lax.broadcasted_iota(jnp.int32, (1, 128), 1)
    lane32 = lax.broadcasted_iota(jnp.int32, (1, BLOCKS), 1)
    blk_col = lax.broadcasted_iota(jnp.int32, (BLOCKS, 1), 0)
    for copy in tables:
        copy.wait()
    layer_row = layer_v[...]
    owner_row = owner_v[...]
    layer_col = jnp.sum(jnp.where(row // 8 == lane32, layer_row, 0), axis=1, keepdims=True)
    in_layer = (lane256 // RANK) == layer_col
    low = lane128 < RANK
    owner_col = jnp.sum(jnp.where(blk_col == lane32, owner_row, 0), axis=1, keepdims=True)
    same = owner_col == owner_row
    slot_col = owner_col * 2 + jnp.sum(
        jnp.where(same & (lane32 < blk_col), 1, 0), axis=1, keepdims=True
    )
    layer_blk = jnp.sum(jnp.where(blk_col == lane32, layer_row, 0), axis=1, keepdims=True)
    entry = jnp.where(blk_col == lane128, slot_col, 0)
    for j in range(2):
        hit = slot_col == me * 2 + j
        entry = entry + jnp.where(hit & (lane128 == 32 + j), layer_blk, 0)
        entry = entry + jnp.where(hit & (lane128 == 34 + j), 1, 0)
    table[...] = jnp.sum(entry, axis=0, keepdims=True)

    copies[8].wait()
    for t in range(D // TILE):
        cols = slice(t * TILE, (t + 1) * TILE)
        high, low_part = split(bt[:, :, cols])
        for k, term in enumerate((high, low_part, high, low_part)):
            terms[:, k * RANK:(k + 1) * RANK, cols] = term

    def basis_terms(cols):
        return [terms[:, k * RANK:(k + 1) * RANK, cols].reshape(256, TILE) for k in range(2)]

    for copy in onward[14:] + direct[:FIRST]:
        copy.start()
    copies[9].wait()
    every = jnp.zeros((256, 256), F32)
    for t in range(D // TILE):
        cols = slice(t * TILE, (t + 1) * TILE)
        high, low_part = split(d[:, cols])
        along = ((1,), (1,))
        bt_high, bt_low = basis_terms(cols)
        every = every + (
            dot(high, bt_high, along) + (dot(high, bt_low, along) + dot(low_part, bt_high, along))
        )
    every = jnp.where(in_layer, every, 0.0)
    both = every[:, :128] + every[:, 128:]
    both = both + pltpu.roll(both, RANK, 1)
    parts[rep] = jnp.where(low, both[:128], both[128:])

    slot_lane = jnp.sum(jnp.where(lane256 // 8 == blk_col, slot_col, 0), axis=0, keepdims=True)
    same_row = (row % 8) == (lane256 % 8)
    pick = [
        jnp.where(((row // 8) * 2 + j == slot_lane) & same_row, 1.0, 0.0) for j in range(2)
    ]

    part_copies = [
        send(parts.at[rep], parts.at[rep], part_send.at[k], part_recv.at[k], to)
        for k, to in enumerate(peers)
    ]
    for copy in part_copies[1:] + part_copies[:1]:
        copy.start()

    for i in range(9):
        onward_step(i)
    for copy in part_copies:
        copy.wait_recv()
    averaged = ((parts[0] + parts[1]) + (parts[2] + parts[3])) * 0.25
    turned = pltpu.roll(averaged, RANK, 1)
    dup = jnp.concatenate(
        [jnp.where(low, averaged, turned), jnp.where(low, turned, averaged)], axis=0
    )
    chosen = [
        jnp.dot(p, dup, precision=HIGHEST, preferred_element_type=F32) for p in pick
    ]
    packed[...] = jnp.where(low, chosen[0], chosen[1]).reshape(OWN, 8, 128)

    def spread(pairs, keep):
        return jnp.where(keep, jnp.concatenate([pairs, pairs], axis=1), 0.0)

    og_high, og_low = split(spread(dup, in_layer))

    takes = core == (lo + y + z + 1) % 2

    def send_tiles(parity):
        for dy, dz in NEAR[::-1] + [(0, 0)]:
            for s in range(2):
                if (dy + dz + s) % 2 != parity or (s == 0 and (dy, dz) == (0, 0)):
                    continue
                ty, tz = (y + dy) % 4, (z + dz) % 4
                to_lo = lo if s == 0 else 1 - lo
                send(
                    packed.at[to_lo * 16 + tz * 4 + ty], placed.at[me], packed_send.at[0],
                    packed_recv.at[0], device(hi * 2 + to_lo, ty, tz, core),
                ).start()

    own_packed = pltpu.make_async_copy(packed.at[me], placed.at[me], own_sem.at[1])

    @pl.when(takes)
    def _():
        own_packed.start()
        send_tiles(0)

    @pl.when(jnp.logical_not(takes))
    def _():
        send_tiles(1)

    for copy in direct[FIRST:]:
        copy.start()

    for i in range(9, 15):
        onward_step(i)

    def og_body(t, carry):
        cols = pl.ds(pl.multiple_of(t * TILE, TILE), TILE)
        bt_high, bt_low = basis_terms(cols)
        og[:, cols] = dot(og_high, bt_high) + (dot(og_high, bt_low) + dot(og_low, bt_high))
        return carry

    lax.fori_loop(0, D // TILE, og_body, 0)
    steps = {"side": side_step, "swap": swap_step}
    hand_over = send(placed, placed, packed_send.at[1], packed_recv.at[1], partner)
    tiles = [
        send(packed.at[pl.ds(0, n)], placed.at[pl.ds(0, n)], packed_send.at[0], packed_recv.at[0], up)
        for n in (15, 16, 31)
    ]
    late = 9
    for kind, i in PASSES[:-late]:
        steps[kind](i)

    @pl.when(takes)
    def _():
        own_packed.wait()
        tiles[2].wait_recv()
        hand_over.start()

    for kind, i in PASSES[-late:]:
        steps[kind](i)

    @pl.when(jnp.logical_not(takes))
    def _():
        hand_over.wait_recv()

    copies[10].wait()
    copies[11].wait()
    own_copy.wait()
    for i in range(32):
        send(r.at[0, 0], r.at[other, 0], swap_send, swap_recv.at[i], partner).wait_recv()

    flat = r.at[0]
    send(flat.at[pl.ds(0, 15)], flat.at[pl.ds(0, 15)], far_send, far_recv.at[0], up).wait_send()
    send(relay.at[pl.ds(0, 15)], relay.at[pl.ds(0, 15)], relay_send, far_recv.at[0], up).wait_send()
    send(flat.at[pl.ds(0, 16)], flat.at[pl.ds(0, 16)], side_send, far_recv.at[0], up).wait_send()
    send(flat, flat, swap_send, far_recv.at[0], up).wait_send()
    for copy in part_copies:
        copy.wait_send()

    @pl.when(takes)
    def _():
        tiles[0].wait_send()
        hand_over.wait_send()

    @pl.when(jnp.logical_not(takes))
    def _():
        tiles[1].wait_send()


def finish(
    w, m, r, og, placed, terms, table_v, new_weights, new_momentum, replica,
    moved_w, moved_m, rows, table, sem, row_sem, table_sem,
):
    table_copy = pltpu.make_async_copy(table_v, table, table_sem)
    table_copy.start()
    got = placed[...].reshape(256, 128)
    got_turned = pltpu.roll(got, RANK, 1)
    lane = lax.broadcasted_iota(jnp.int32, (1, 128), 1)
    low = lane < RANK
    sides = []
    for j in range(2):
        pairs = jnp.where(low, got, got_turned) if j == 0 else jnp.where(low, got_turned, got)
        sides.append(jnp.concatenate(split(pairs), axis=1))

    copies = []

    def issue(k):
        for copy in copies[2 * k:2 * k + 2]:
            copy.start()

    for j in range(2):
        layer = jnp.sum(jnp.where(lane == 32 + j, table_v[...], 0))
        use = jnp.where(lane == 34 + j, table_v[...], 0)
        use = jnp.sum(use, axis=1, keepdims=True).astype(F32)
        for t in range(D // TILE):
            cols = slice(t * TILE, (t + 1) * TILE)
            k = j * (D // TILE) + t
            grad = dot(sides[j], terms[layer, :, cols])
            moved = (momentum_decay * m[j, :, :, :, :, cols].reshape(256, TILE) + grad) * use
            moved_m[j, :, cols] = moved
            moved_w[j, :, cols] = (
                w[j, :, :, :, :, cols].reshape(256, TILE)
                - outer_rate * (grad + momentum_decay * moved)
            ) * use
            copies.append(pltpu.make_async_copy(
                moved_m.at[j, :, cols], new_momentum.at[j, :, cols], sem.at[0, k]))
            copies.append(pltpu.make_async_copy(
                moved_w.at[j, :, cols], new_weights.at[j, :, cols], sem.at[1, k]))
            if k > 0:
                issue(k - 1)

    def out_body(b, carry):
        slot = table[0, b]
        for half in range(2):
            cols = slice(half * HALF, (half + 1) * HALF)
            rows[b, :, cols] = r[half, slot // 2, slot % 2] - (
                outer_rate * (1.0 + momentum_decay)
            ) * og[pl.ds(pl.multiple_of(b * 8, 8), 8), cols]
        return carry

    row_copies = [
        pltpu.make_async_copy(rows.at[pl.ds(g * 8, 8)], replica.at[pl.ds(g * 8, 8)], row_sem.at[g])
        for g in range(4)
    ]
    table_copy.wait()
    for g in range(4):
        lax.fori_loop(g * 8, g * 8 + 8, out_body, 0)
        if g == 0:
            issue(2 * (D // TILE) - 1)
        else:
            row_copies[g - 1].start()
    row_copies[3].start()
    for copy in copies + row_copies:
        copy.wait()


def local(replica_delta, layer_basis, layer_of, owner_of, weights_owned, momentum_owned):
    vmem = pl.BlockSpec(memory_space=pltpu.VMEM)
    hbm = pl.BlockSpec(memory_space=pltpu.HBM)
    dma = pltpu.SemaphoreType.DMA
    basis = jnp.swapaxes(layer_basis, 1, 2)
    delta = replica_delta.reshape(256, D)
    weights = weights_owned.reshape(2, 2, 4, 4, 8, D)
    momentum = momentum_owned.reshape(2, 2, 4, 4, 8, D)
    between = pl.pallas_call(
        exchange,
        out_shape=(
            pltpu.VMEM((2, 2, 4, 4, 8, D), F32),
            pltpu.VMEM((2, 2, 4, 4, 8, D), F32),
            pltpu.VMEM((2, OWN, 2, 8, HALF), F32),
            pltpu.VMEM((256, D), F32),
            pltpu.VMEM((OWN, 8, 128), F32),
            pltpu.VMEM((4, 4 * RANK, D), BF16),
            pltpu.VMEM((1, 128), jnp.int32),
        ),
        in_specs=[hbm] * 6,
        out_specs=(vmem,) * 7,
        scratch_shapes=[
            pltpu.VMEM((1, BLOCKS), jnp.int32),
            pltpu.VMEM((1, BLOCKS), jnp.int32),
            pltpu.VMEM((256, D), F32),
            pltpu.VMEM((4, RANK, D), F32),
            pltpu.VMEM((2, 4, 4, 2, 8, HALF), F32),
            pltpu.VMEM((16, 8, HALF), F32),
            pltpu.VMEM((4, 128, 128), F32),
            pltpu.VMEM((OWN, 8, 128), F32),
            dma((12,)),
            dma, dma((15,)),
            dma, dma((15,)),
            dma, dma((2, 16)),
            dma, dma((32,)),
            dma((3,)), dma((3,)),
            dma((2,)), dma((2,)),
            dma((2,)),
            dma((2,)),
        ],
        compiler_params=pltpu.CompilerParams(
            collective_id=0, has_side_effects=True, vmem_limit_bytes=45 << 20
        ),
        name="outer_step",
    )(owner_of.reshape(1, BLOCKS), layer_of.reshape(1, BLOCKS), delta, basis, weights, momentum)
    shapes = ((2, 256, D), (2, 256, D), (BLOCKS, 8, D))
    return pl.pallas_call(
        finish,
        out_shape=tuple(jax.ShapeDtypeStruct(shape, F32) for shape in shapes),
        in_specs=[vmem] * 7,
        out_specs=(hbm,) * 3,
        scratch_shapes=[
            pltpu.VMEM((2, 256, D), F32), pltpu.VMEM((2, 256, D), F32),
            pltpu.VMEM((BLOCKS, 8, D), F32), pltpu.SMEM((1, 128), jnp.int32),
            dma((2, 14)), dma((4,)), dma,
        ],
        compiler_params=pltpu.CompilerParams(vmem_limit_bytes=16 << 20),
        name="finish",
    )(*between)


def solution(mesh):
    placed = (
        P("rep", None, "own", None),
        P(),
        P(),
        P(),
        P("own", None, None),
        P("own", None, None),
    )
    return jax.shard_map(
        local,
        mesh=mesh,
        in_specs=placed,
        out_specs=(P("own", None, None), P("own", None, None), P(None, "own", None)),
        check_vma=False,
    )
```

```python
import jax
import jax.numpy as jnp
from jax import lax
from jax.experimental import pallas as pl
from jax.experimental.pallas import tpu as pltpu
from jax.sharding import PartitionSpec as P

momentum_decay = 0.9
outer_rate = 0.7

MESH = pl.DeviceIdType.MESH
HIGHEST = lax.Precision.HIGHEST
D = 1792
HALF = D // 2
RANK = 64
BLOCKS = 32
OWN = 32
TILE = 256
BF16 = jnp.bfloat16
F32 = jnp.float32

DZ = [0, 1, 3, 2]
NEAR = [(1, 0), (3, 0), (0, 1), (0, 3),
        (2, 0), (1, 1), (3, 3), (3, 1), (1, 3), (0, 2),
        (1, 2), (3, 2), (2, 1), (2, 3), (2, 2)]
FAR = [(1, 0), (3, 0), (0, 1), (0, 3),
       (2, 2), (1, 2), (3, 2), (2, 1), (2, 3),
       (1, 1), (3, 3), (3, 1), (1, 3), (2, 0), (0, 2)]
FIRST = 9
GROUP_AT = (7, 9, 11, 12)
PASSES = [("swap", i) for i in range(4)] + [("side", 15)] + [("side", i) for i in range(4)]
PASSES += [("side", i) for i in range(4, 8)]
PASSES += [("swap", i) for i in range(4, 9)] + [("side", i) for i in range(8, 12)]
PASSES += [("swap", i) for i in range(9, 12)]
PASSES += [("side", i) for i in range(12, 15)] + [("swap", i) for i in range(12, 15)]


def place():
    rep = lax.axis_index("rep")
    own = lax.axis_index("own")
    x = (rep // 2) * 2 + own // 16
    return x, own % 4, (own // 4) % 4, rep % 2


def device(x, y, z, core):
    return ((x // 2) * 2 + core, (x % 2) * 16 + z * 4 + y)


def send(src, dst, send_sem, recv_sem, to):
    return pltpu.make_async_remote_copy(
        src_ref=src, dst_ref=dst, send_sem=send_sem, recv_sem=recv_sem,
        device_id=to, device_id_type=MESH,
    )


def split(value):
    high = value.astype(BF16)
    return high, (value - high.astype(F32)).astype(BF16)


def dot(a, b, dims=((1,), (0,))):
    return lax.dot_general(a, b, (dims, ((), ())), preferred_element_type=F32)


def exchange(
    owner_hbm, layer_hbm, delta_hbm, basis_hbm, weights_hbm, momentum_hbm,
    w, m, r, og, placed, terms, table,
    owner_v, layer_v, d, bt, q, relay, parts, packed,
    load_sem, far_send, far_recv, relay_send, relay_recv, side_send, side_recv,
    swap_send, swap_recv, part_send, part_recv, packed_send, packed_recv, own_sem,
    table_sem,
):
    x, y, z, core = place()
    lo, hi = x % 2, x // 2
    rep = hi * 2 + core
    me = lo * 16 + z * 4 + y
    other = 1 - core
    x_up, x_down, x_far = (x + 1) % 4, (x + 3) % 4, (x + 2) % 4
    up, down = device(x_up, y, z, core), device(x_down, y, z, core)
    partner = device(x, y, z, other)
    peers = [partner, device(x_far, y, z, core), device(x_far, y, z, other)]

    barrier = pltpu.get_barrier_semaphore()
    targets = []
    for dy, dz in reversed(NEAR):
        for tx in (hi * 2 + 1 - lo, x):
            targets.append(device(tx, (y + dy) % 4, (z + dz) % 4, core))
    targets += peers + [up, down]
    for to in targets:
        pl.semaphore_signal(barrier, inc=1, device_id=to, device_id_type=MESH)

    tables = [
        pltpu.make_async_copy(a, b, table_sem.at[i])
        for i, (a, b) in enumerate(((owner_hbm, owner_v), (layer_hbm, layer_v)))
    ]
    for copy in tables:
        copy.start()

    mine = pl.ds(pl.multiple_of(core * HALF, 128), HALF)
    rest = pl.ds(pl.multiple_of(other * HALF, 128), HALF)
    loads = []
    for dz in DZ:
        tz = (z + dz) % 4
        loads.append((weights_hbm.at[:, :, tz, :, :, mine], w.at[:, :, tz, :, :, mine]))
        loads.append((momentum_hbm.at[:, :, tz, :, :, mine], m.at[:, :, tz, :, :, mine]))
    loads += [
        (basis_hbm, bt),
        (delta_hbm, d),
        (weights_hbm.at[:, :, :, :, :, rest], w.at[:, :, :, :, :, rest]),
        (momentum_hbm.at[:, :, :, :, :, rest], m.at[:, :, :, :, :, rest]),
    ]
    copies = [pltpu.make_async_copy(a, b, load_sem.at[i]) for i, (a, b) in enumerate(loads)]
    for copy in copies:
        copy.start()

    def q_rows(k):
        tz = (z + DZ[k]) % 4
        copies[2 * k].wait()
        copies[2 * k + 1].wait()
        for half in range(2):
            @pl.when(core == half)
            def _():
                cols = slice(half * HALF, (half + 1) * HALF)
                for s in range(2):
                    q[:, tz, :, s] = w[s, :, tz, :, :, cols] - (
                        outer_rate * momentum_decay * momentum_decay
                    ) * m[s, :, tz, :, :, cols]

    def direct_copy(i):
        dy, dz = FAR[i]
        ty, tz = (y + dy) % 4, (z + dz) % 4
        return send(
            q.at[lo, tz, ty], r.at[core, me], far_send, far_recv.at[i], device(x, ty, tz, core)
        )

    def onward_copy(i):
        dy, dz = NEAR[i]
        ty, tz = (y + dy) % 4, (z + dz) % 4
        return send(
            q.at[1 - lo, tz, ty, hi], relay.at[z * 4 + y], relay_send, relay_recv.at[i],
            device(x, ty, tz, core),
        )

    onward = [onward_copy(i) for i in range(15)]
    direct = [direct_copy(i) for i in range(15)]
    own_copy = pltpu.make_async_copy(q.at[lo, z, y], r.at[core, me], own_sem.at[0])
    own_swap = send(q.at[lo, z, y], r.at[core, me], swap_send, swap_recv.at[15], partner)
    side = [
        send(q.at[1 - lo, z, y, hi], r.at[core, me, hi], side_send, side_recv.at[k, 15], to)
        for k, to in enumerate((up, down))
    ]

    q_rows(0)
    q_rows(1)
    pl.semaphore_wait(barrier, len(targets))
    for copy in side + onward[:2]:
        copy.start()
    q_rows(2)
    onward[2].start()
    q_rows(3)
    for copy in onward[3:14]:
        copy.start()
    own_copy.start()
    own_swap.start()

    def source(dy, dz):
        return (y + 4 - dy) % 4, (z + 4 - dz) % 4

    def onward_step(i):
        fy, fz = source(*NEAR[i])
        src = lo * 16 + fz * 4 + fy
        onward[i].wait_recv()
        for k, to in enumerate((up, down)):
            send(relay.at[fz * 4 + fy], r.at[core, src, hi], side_send, side_recv.at[k, i], to).start()

    def swap_step(i):
        fy, fz = source(*FAR[i])
        src = lo * 16 + fz * 4 + fy
        direct[i].wait_recv()
        send(r.at[core, src], r.at[core, src], swap_send, swap_recv.at[i], partner).start()

    def side_step(i):
        fy, fz = source(*(NEAR[i] if i < 15 else (0, 0)))
        src = (1 - lo) * 16 + fz * 4 + fy
        for k, from_x in enumerate((x_down, x_up)):
            send(
                relay.at[0], r.at[core, src, from_x // 2], side_send, side_recv.at[k, i], up
            ).wait_recv()
        send(r.at[core, src], r.at[core, src], swap_send, swap_recv.at[16 + i], partner).start()

    row = lax.broadcasted_iota(jnp.int32, (256, 1), 0)
    lane256 = lax.broadcasted_iota(jnp.int32, (1, 256), 1)
    lane128 = lax.broadcasted_iota(jnp.int32, (1, 128), 1)
    lane32 = lax.broadcasted_iota(jnp.int32, (1, BLOCKS), 1)
    blk_col = lax.broadcasted_iota(jnp.int32, (BLOCKS, 1), 0)
    for copy in tables:
        copy.wait()
    layer_row = layer_v[...]
    owner_row = owner_v[...]
    layer_col = jnp.sum(jnp.where(row // 8 == lane32, layer_row, 0), axis=1, keepdims=True)
    in_layer = (lane256 // RANK) == layer_col
    low = lane128 < RANK
    owner_col = jnp.sum(jnp.where(blk_col == lane32, owner_row, 0), axis=1, keepdims=True)
    same = owner_col == owner_row
    slot_col = owner_col * 2 + jnp.sum(
        jnp.where(same & (lane32 < blk_col), 1, 0), axis=1, keepdims=True
    )
    layer_blk = jnp.sum(jnp.where(blk_col == lane32, layer_row, 0), axis=1, keepdims=True)
    entry = jnp.where(blk_col == lane128, slot_col, 0)
    for j in range(2):
        hit = slot_col == me * 2 + j
        entry = entry + jnp.where(hit & (lane128 == 32 + j), layer_blk, 0)
        entry = entry + jnp.where(hit & (lane128 == 34 + j), 1, 0)
    table[...] = jnp.sum(entry, axis=0, keepdims=True)

    copies[8].wait()
    for t in range(D // TILE):
        cols = slice(t * TILE, (t + 1) * TILE)
        high, low_part = split(bt[:, :, cols])
        for k, term in enumerate((high, low_part, high, low_part)):
            terms[:, k * RANK:(k + 1) * RANK, cols] = term

    def basis_terms(cols):
        return [terms[:, k * RANK:(k + 1) * RANK, cols].reshape(256, TILE) for k in range(2)]

    for copy in onward[14:] + direct[:FIRST]:
        copy.start()
    copies[9].wait()
    every = jnp.zeros((256, 256), F32)
    for t in range(D // TILE):
        cols = slice(t * TILE, (t + 1) * TILE)
        high, low_part = split(d[:, cols])
        along = ((1,), (1,))
        bt_high, bt_low = basis_terms(cols)
        every = every + (
            dot(high, bt_high, along) + (dot(high, bt_low, along) + dot(low_part, bt_high, along))
        )
    every = jnp.where(in_layer, every, 0.0)
    both = every[:, :128] + every[:, 128:]
    both = both + pltpu.roll(both, RANK, 1)
    parts[rep] = jnp.where(low, both[:128], both[128:])

    slot_lane = jnp.sum(jnp.where(lane256 // 8 == blk_col, slot_col, 0), axis=0, keepdims=True)
    same_row = (row % 8) == (lane256 % 8)
    pick = [
        jnp.where(((row // 8) * 2 + j == slot_lane) & same_row, 1.0, 0.0) for j in range(2)
    ]

    part_copies = [
        send(parts.at[rep], parts.at[rep], part_send.at[k], part_recv.at[k], to)
        for k, to in enumerate(peers)
    ]
    for copy in part_copies[1:] + part_copies[:1]:
        copy.start()

    for i in range(9):
        onward_step(i)
    for copy in part_copies:
        copy.wait_recv()
    averaged = ((parts[0] + parts[1]) + (parts[2] + parts[3])) * 0.25
    turned = pltpu.roll(averaged, RANK, 1)
    dup = jnp.concatenate(
        [jnp.where(low, averaged, turned), jnp.where(low, turned, averaged)], axis=0
    )
    chosen = [
        jnp.dot(p, dup, precision=HIGHEST, preferred_element_type=F32) for p in pick
    ]
    packed[...] = jnp.where(low, chosen[0], chosen[1]).reshape(OWN, 8, 128)

    def spread(pairs, keep):
        return jnp.where(keep, jnp.concatenate([pairs, pairs], axis=1), 0.0)

    og_high, og_low = split(spread(dup, in_layer))

    takes = core == (lo + y + z + 1) % 2

    def send_tiles(parity):
        for dy, dz in NEAR[::-1] + [(0, 0)]:
            for s in range(2):
                if (dy + dz + s) % 2 != parity or (s == 0 and (dy, dz) == (0, 0)):
                    continue
                ty, tz = (y + dy) % 4, (z + dz) % 4
                to_lo = lo if s == 0 else 1 - lo
                send(
                    packed.at[to_lo * 16 + tz * 4 + ty], placed.at[me], packed_send.at[0],
                    packed_recv.at[0], device(hi * 2 + to_lo, ty, tz, core),
                ).start()

    own_packed = pltpu.make_async_copy(packed.at[me], placed.at[me], own_sem.at[1])

    @pl.when(takes)
    def _():
        own_packed.start()
        send_tiles(0)

    @pl.when(jnp.logical_not(takes))
    def _():
        send_tiles(1)

    for copy in direct[FIRST:]:
        copy.start()

    for i in range(9, 15):
        onward_step(i)

    def og_body(t, carry):
        cols = pl.ds(pl.multiple_of(t * TILE, TILE), TILE)
        bt_high, bt_low = basis_terms(cols)
        og[:, cols] = dot(og_high, bt_high) + (dot(og_high, bt_low) + dot(og_low, bt_high))
        return carry

    lax.fori_loop(0, D // TILE, og_body, 0)
    steps = {"side": side_step, "swap": swap_step}
    hand_over = send(placed, placed, packed_send.at[1], packed_recv.at[1], partner)
    tiles = [
        send(packed.at[pl.ds(0, n)], placed.at[pl.ds(0, n)], packed_send.at[0], packed_recv.at[0], up)
        for n in (15, 16, 31)
    ]
    late = 9
    for kind, i in PASSES[:-late]:
        steps[kind](i)

    @pl.when(takes)
    def _():
        own_packed.wait()
        tiles[2].wait_recv()
        hand_over.start()

    for kind, i in PASSES[-late:]:
        steps[kind](i)

    @pl.when(jnp.logical_not(takes))
    def _():
        hand_over.wait_recv()

    copies[10].wait()
    copies[11].wait()
    own_copy.wait()
    for i in range(32):
        send(r.at[0, 0], r.at[other, 0], swap_send, swap_recv.at[i], partner).wait_recv()

    flat = r.at[0]
    send(flat.at[pl.ds(0, 15)], flat.at[pl.ds(0, 15)], far_send, far_recv.at[0], up).wait_send()
    send(relay.at[pl.ds(0, 15)], relay.at[pl.ds(0, 15)], relay_send, far_recv.at[0], up).wait_send()
    send(flat.at[pl.ds(0, 16)], flat.at[pl.ds(0, 16)], side_send, far_recv.at[0], up).wait_send()
    send(flat, flat, swap_send, far_recv.at[0], up).wait_send()
    for copy in part_copies:
        copy.wait_send()

    @pl.when(takes)
    def _():
        tiles[0].wait_send()
        hand_over.wait_send()

    @pl.when(jnp.logical_not(takes))
    def _():
        tiles[1].wait_send()


def finish(
    w, m, r, og, placed, terms, table_v, new_weights, new_momentum, replica,
    moved_w, moved_m, rows, table, sem, row_sem, table_sem,
):
    table_copy = pltpu.make_async_copy(table_v, table, table_sem)
    table_copy.start()
    got = placed[...].reshape(256, 128)
    got_turned = pltpu.roll(got, RANK, 1)
    lane = lax.broadcasted_iota(jnp.int32, (1, 128), 1)
    low = lane < RANK
    sides = []
    for j in range(2):
        pairs = jnp.where(low, got, got_turned) if j == 0 else jnp.where(low, got_turned, got)
        sides.append(jnp.concatenate(split(pairs), axis=1))

    copies = []

    def issue(k):
        for copy in copies[2 * k:2 * k + 2]:
            copy.start()

    def out_body(b, carry):
        slot = table[0, b]
        for half in range(2):
            cols = slice(half * HALF, (half + 1) * HALF)
            rows[b, :, cols] = r[half, slot // 2, slot % 2] - (
                outer_rate * (1.0 + momentum_decay)
            ) * og[pl.ds(pl.multiple_of(b * 8, 8), 8), cols]
        return carry

    row_copies = [
        pltpu.make_async_copy(rows.at[pl.ds(g * 8, 8)], replica.at[pl.ds(g * 8, 8)], row_sem.at[g])
        for g in range(4)
    ]
    for j in range(2):
        layer = jnp.sum(jnp.where(lane == 32 + j, table_v[...], 0))
        use = jnp.where(lane == 34 + j, table_v[...], 0)
        use = jnp.sum(use, axis=1, keepdims=True).astype(F32)
        for t in range(D // TILE):
            cols = slice(t * TILE, (t + 1) * TILE)
            k = j * (D // TILE) + t
            grad = dot(sides[j], terms[layer, :, cols])
            moved = (momentum_decay * m[j, :, :, :, :, cols].reshape(256, TILE) + grad) * use
            moved_m[j, :, cols] = moved
            moved_w[j, :, cols] = (
                w[j, :, :, :, :, cols].reshape(256, TILE)
                - outer_rate * (grad + momentum_decay * moved)
            ) * use
            copies.append(pltpu.make_async_copy(
                moved_m.at[j, :, cols], new_momentum.at[j, :, cols], sem.at[0, k]))
            copies.append(pltpu.make_async_copy(
                moved_w.at[j, :, cols], new_weights.at[j, :, cols], sem.at[1, k]))
            if k > 0:
                issue(k - 1)
            if k in GROUP_AT:
                g = GROUP_AT.index(k)
                if g == 0:
                    table_copy.wait()
                else:
                    row_copies[g - 1].start()
                lax.fori_loop(g * 8, g * 8 + 8, out_body, 0)
    issue(2 * (D // TILE) - 1)

    row_copies[3].start()
    for copy in copies + row_copies:
        copy.wait()


def local(replica_delta, layer_basis, layer_of, owner_of, weights_owned, momentum_owned):
    vmem = pl.BlockSpec(memory_space=pltpu.VMEM)
    hbm = pl.BlockSpec(memory_space=pltpu.HBM)
    dma = pltpu.SemaphoreType.DMA
    basis = jnp.swapaxes(layer_basis, 1, 2)
    delta = replica_delta.reshape(256, D)
    weights = weights_owned.reshape(2, 2, 4, 4, 8, D)
    momentum = momentum_owned.reshape(2, 2, 4, 4, 8, D)
    between = pl.pallas_call(
        exchange,
        out_shape=(
            pltpu.VMEM((2, 2, 4, 4, 8, D), F32),
            pltpu.VMEM((2, 2, 4, 4, 8, D), F32),
            pltpu.VMEM((2, OWN, 2, 8, HALF), F32),
            pltpu.VMEM((256, D), F32),
            pltpu.VMEM((OWN, 8, 128), F32),
            pltpu.VMEM((4, 4 * RANK, D), BF16),
            pltpu.VMEM((1, 128), jnp.int32),
        ),
        in_specs=[hbm] * 6,
        out_specs=(vmem,) * 7,
        scratch_shapes=[
            pltpu.VMEM((1, BLOCKS), jnp.int32),
            pltpu.VMEM((1, BLOCKS), jnp.int32),
            pltpu.VMEM((256, D), F32),
            pltpu.VMEM((4, RANK, D), F32),
            pltpu.VMEM((2, 4, 4, 2, 8, HALF), F32),
            pltpu.VMEM((16, 8, HALF), F32),
            pltpu.VMEM((4, 128, 128), F32),
            pltpu.VMEM((OWN, 8, 128), F32),
            dma((12,)),
            dma, dma((15,)),
            dma, dma((15,)),
            dma, dma((2, 16)),
            dma, dma((32,)),
            dma((3,)), dma((3,)),
            dma((2,)), dma((2,)),
            dma((2,)),
            dma((2,)),
        ],
        compiler_params=pltpu.CompilerParams(
            collective_id=0, has_side_effects=True, vmem_limit_bytes=45 << 20
        ),
        name="outer_step",
    )(owner_of.reshape(1, BLOCKS), layer_of.reshape(1, BLOCKS), delta, basis, weights, momentum)
    shapes = ((2, 256, D), (2, 256, D), (BLOCKS, 8, D))
    return pl.pallas_call(
        finish,
        out_shape=tuple(jax.ShapeDtypeStruct(shape, F32) for shape in shapes),
        in_specs=[vmem] * 7,
        out_specs=(hbm,) * 3,
        scratch_shapes=[
            pltpu.VMEM((2, 256, D), F32), pltpu.VMEM((2, 256, D), F32),
            pltpu.VMEM((BLOCKS, 8, D), F32), pltpu.SMEM((1, 128), jnp.int32),
            dma((2, 14)), dma((4,)), dma,
        ],
        compiler_params=pltpu.CompilerParams(vmem_limit_bytes=16 << 20),
        name="finish",
    )(*between)


def solution(mesh):
    placed = (
        P("rep", None, "own", None),
        P(),
        P(),
        P(),
        P("own", None, None),
        P("own", None, None),
    )
    return jax.shard_map(
        local,
        mesh=mesh,
        in_specs=placed,
        out_specs=(P("own", None, None), P("own", None, None), P(None, "own", None)),
        check_vma=False,
    )
```

```python
import jax
import jax.numpy as jnp
from jax import lax
from jax.experimental import pallas as pl
from jax.experimental.pallas import tpu as pltpu
from jax.sharding import PartitionSpec as P

momentum_decay = 0.9
outer_rate = 0.7

MESH = pl.DeviceIdType.MESH
D = 1792
HALF = D // 2
RANK = 64
BLOCKS = 32
OWN = 32
TILE = 256
BF16 = jnp.bfloat16
F32 = jnp.float32

DZ = [0, 1, 3, 2]
NEAR = [(1, 0), (3, 0), (0, 1), (0, 3),
        (2, 0), (1, 1), (3, 3), (3, 1), (1, 3), (0, 2),
        (1, 2), (3, 2), (2, 1), (2, 3), (2, 2)]
FAR = [(1, 0), (3, 0), (0, 1), (0, 3),
       (2, 2), (1, 2), (3, 2), (2, 1), (2, 3),
       (1, 1), (3, 3), (3, 1), (1, 3), (2, 0), (0, 2)]
FIRST = 9
GROUP_AT = (7, 9, 11, 12)
PASSES = [("swap", i) for i in range(4)] + [("side", 15)] + [("side", i) for i in range(4)]
PASSES += [("side", i) for i in range(4, 8)]
PASSES += [("swap", i) for i in range(4, 9)] + [("side", i) for i in range(8, 12)]
PASSES += [("swap", i) for i in range(9, 12)]
PASSES += [("side", i) for i in range(12, 15)] + [("swap", i) for i in range(12, 15)]


def place():
    rep = lax.axis_index("rep")
    own = lax.axis_index("own")
    x = (rep // 2) * 2 + own // 16
    return x, own % 4, (own // 4) % 4, rep % 2


def device(x, y, z, core):
    return ((x // 2) * 2 + core, (x % 2) * 16 + z * 4 + y)


def send(src, dst, send_sem, recv_sem, to):
    return pltpu.make_async_remote_copy(
        src_ref=src, dst_ref=dst, send_sem=send_sem, recv_sem=recv_sem,
        device_id=to, device_id_type=MESH,
    )


def split(value):
    high = value.astype(BF16)
    return high, (value - high.astype(F32)).astype(BF16)


def dot(a, b, dims=((1,), (0,))):
    return lax.dot_general(a, b, (dims, ((), ())), preferred_element_type=F32)


def exchange(
    owner_hbm, layer_hbm, delta_hbm, basis_hbm, weights_hbm, momentum_hbm,
    w, m, r, og, placed, terms, table,
    owner_v, layer_v, d, bt, q, relay, parts, packed,
    load_sem, far_send, far_recv, relay_send, relay_recv, side_send, side_recv,
    swap_send, swap_recv, part_send, part_recv, packed_send, packed_recv, own_sem,
    table_sem,
):
    x, y, z, core = place()
    lo, hi = x % 2, x // 2
    rep = hi * 2 + core
    me = lo * 16 + z * 4 + y
    other = 1 - core
    x_up, x_down, x_far = (x + 1) % 4, (x + 3) % 4, (x + 2) % 4
    up, down = device(x_up, y, z, core), device(x_down, y, z, core)
    partner = device(x, y, z, other)
    peers = [partner, device(x_far, y, z, core), device(x_far, y, z, other)]

    barrier = pltpu.get_barrier_semaphore()
    targets = []
    for dy, dz in reversed(NEAR):
        for tx in (hi * 2 + 1 - lo, x):
            targets.append(device(tx, (y + dy) % 4, (z + dz) % 4, core))
    targets += peers + [up, down]
    for to in targets:
        pl.semaphore_signal(barrier, inc=1, device_id=to, device_id_type=MESH)

    tables = [
        pltpu.make_async_copy(a, b, table_sem.at[i])
        for i, (a, b) in enumerate(((owner_hbm, owner_v), (layer_hbm, layer_v)))
    ]
    for copy in tables:
        copy.start()

    mine = pl.ds(pl.multiple_of(core * HALF, 128), HALF)
    rest = pl.ds(pl.multiple_of(other * HALF, 128), HALF)
    loads = []
    for dz in DZ:
        tz = (z + dz) % 4
        loads.append((weights_hbm.at[:, :, tz, :, :, mine], w.at[:, :, tz, :, :, mine]))
        loads.append((momentum_hbm.at[:, :, tz, :, :, mine], m.at[:, :, tz, :, :, mine]))
    loads += [
        (basis_hbm, bt),
        (delta_hbm, d),
        (weights_hbm.at[:, :, :, :, :, rest], w.at[:, :, :, :, :, rest]),
        (momentum_hbm.at[:, :, :, :, :, rest], m.at[:, :, :, :, :, rest]),
    ]
    copies = [pltpu.make_async_copy(a, b, load_sem.at[i]) for i, (a, b) in enumerate(loads)]
    for copy in copies:
        copy.start()

    def q_rows(k):
        tz = (z + DZ[k]) % 4
        copies[2 * k].wait()
        copies[2 * k + 1].wait()
        for half in range(2):
            @pl.when(core == half)
            def _():
                cols = slice(half * HALF, (half + 1) * HALF)
                for s in range(2):
                    q[:, tz, :, s] = w[s, :, tz, :, :, cols] - (
                        outer_rate * momentum_decay * momentum_decay
                    ) * m[s, :, tz, :, :, cols]

    def direct_copy(i):
        dy, dz = FAR[i]
        ty, tz = (y + dy) % 4, (z + dz) % 4
        return send(
            q.at[lo, tz, ty], r.at[core, me], far_send, far_recv.at[i], device(x, ty, tz, core)
        )

    def onward_copy(i):
        dy, dz = NEAR[i]
        ty, tz = (y + dy) % 4, (z + dz) % 4
        return send(
            q.at[1 - lo, tz, ty, hi], relay.at[z * 4 + y], relay_send, relay_recv.at[i],
            device(x, ty, tz, core),
        )

    onward = [onward_copy(i) for i in range(15)]
    direct = [direct_copy(i) for i in range(15)]
    own_copy = pltpu.make_async_copy(q.at[lo, z, y], r.at[core, me], own_sem.at[0])
    own_swap = send(q.at[lo, z, y], r.at[core, me], swap_send, swap_recv.at[15], partner)
    side = [
        send(q.at[1 - lo, z, y, hi], r.at[core, me, hi], side_send, side_recv.at[k, 15], to)
        for k, to in enumerate((up, down))
    ]

    q_rows(0)
    q_rows(1)
    pl.semaphore_wait(barrier, len(targets))
    for copy in side + onward[:2]:
        copy.start()
    q_rows(2)
    onward[2].start()
    q_rows(3)
    for copy in onward[3:14]:
        copy.start()
    own_copy.start()
    own_swap.start()

    def source(dy, dz):
        return (y + 4 - dy) % 4, (z + 4 - dz) % 4

    def onward_step(i):
        fy, fz = source(*NEAR[i])
        src = lo * 16 + fz * 4 + fy
        onward[i].wait_recv()
        for k, to in enumerate((up, down)):
            send(relay.at[fz * 4 + fy], r.at[core, src, hi], side_send, side_recv.at[k, i], to).start()

    def swap_step(i):
        fy, fz = source(*FAR[i])
        src = lo * 16 + fz * 4 + fy
        direct[i].wait_recv()
        send(r.at[core, src], r.at[core, src], swap_send, swap_recv.at[i], partner).start()

    def side_step(i):
        fy, fz = source(*(NEAR[i] if i < 15 else (0, 0)))
        src = (1 - lo) * 16 + fz * 4 + fy
        for k, from_x in enumerate((x_down, x_up)):
            send(
                relay.at[0], r.at[core, src, from_x // 2], side_send, side_recv.at[k, i], up
            ).wait_recv()
        send(r.at[core, src], r.at[core, src], swap_send, swap_recv.at[16 + i], partner).start()

    row = lax.broadcasted_iota(jnp.int32, (256, 1), 0)
    lane256 = lax.broadcasted_iota(jnp.int32, (1, 256), 1)
    lane128 = lax.broadcasted_iota(jnp.int32, (1, 128), 1)
    lane32 = lax.broadcasted_iota(jnp.int32, (1, BLOCKS), 1)
    blk_col = lax.broadcasted_iota(jnp.int32, (BLOCKS, 1), 0)
    for copy in tables:
        copy.wait()
    layer_row = layer_v[...]
    owner_row = owner_v[...]
    layer_col = jnp.sum(jnp.where(row // 8 == lane32, layer_row, 0), axis=1, keepdims=True)
    in_layer = (lane256 // RANK) == layer_col
    low = lane128 < RANK
    owner_col = jnp.sum(jnp.where(blk_col == lane32, owner_row, 0), axis=1, keepdims=True)
    same = owner_col == owner_row
    slot_col = owner_col * 2 + jnp.sum(
        jnp.where(same & (lane32 < blk_col), 1, 0), axis=1, keepdims=True
    )
    layer_blk = jnp.sum(jnp.where(blk_col == lane32, layer_row, 0), axis=1, keepdims=True)
    entry = jnp.where(blk_col == lane128, slot_col, 0)
    for j in range(2):
        hit = slot_col == me * 2 + j
        entry = entry + jnp.where(hit & (lane128 == 32 + j), layer_blk, 0)
        entry = entry + jnp.where(hit & (lane128 == 34 + j), 1, 0)
    table[...] = jnp.sum(entry, axis=0, keepdims=True)

    copies[8].wait()
    for t in range(D // TILE):
        cols = slice(t * TILE, (t + 1) * TILE)
        high, low_part = split(bt[:, :, cols])
        for k, term in enumerate((high, low_part, high, low_part)):
            terms[:, k * RANK:(k + 1) * RANK, cols] = term

    def basis_terms(cols):
        return [terms[:, k * RANK:(k + 1) * RANK, cols].reshape(256, TILE) for k in range(2)]

    for copy in onward[14:] + direct[:FIRST]:
        copy.start()
    copies[9].wait()
    every = jnp.zeros((256, 256), F32)
    for t in range(D // TILE):
        cols = slice(t * TILE, (t + 1) * TILE)
        high, low_part = split(d[:, cols])
        along = ((1,), (1,))
        bt_high, bt_low = basis_terms(cols)
        every = every + (
            dot(high, bt_high, along) + (dot(high, bt_low, along) + dot(low_part, bt_high, along))
        )
    every = jnp.where(in_layer, every, 0.0)
    both = every[:, :128] + every[:, 128:]
    both = both + pltpu.roll(both, RANK, 1)
    parts[rep] = jnp.where(low, both[:128], both[128:])

    slot_lane = jnp.sum(jnp.where(lane256 // 8 == blk_col, slot_col, 0), axis=0, keepdims=True)
    same_row = (row % 8) == (lane256 % 8)
    pick = [
        jnp.where(((row // 8) * 2 + j == slot_lane) & same_row, 1.0, 0.0).astype(BF16)
        for j in range(2)
    ]

    part_copies = [
        send(parts.at[rep], parts.at[rep], part_send.at[k], part_recv.at[k], to)
        for k, to in enumerate(peers)
    ]
    for copy in part_copies[1:] + part_copies[:1]:
        copy.start()

    for i in range(9):
        onward_step(i)
    for copy in part_copies:
        copy.wait_recv()
    averaged = ((parts[0] + parts[1]) + (parts[2] + parts[3])) * 0.25
    turned = pltpu.roll(averaged, RANK, 1)
    dup = jnp.concatenate(
        [jnp.where(low, averaged, turned), jnp.where(low, turned, averaged)], axis=0
    )
    dup_high, dup_low = split(dup)
    chosen = [dot(p, dup_high) + dot(p, dup_low) for p in pick]
    packed[...] = jnp.where(low, chosen[0], chosen[1]).reshape(OWN, 8, 128)

    def spread(pairs, keep):
        return jnp.where(keep, jnp.concatenate([pairs, pairs], axis=1), 0.0)

    takes = core == (lo + y + z + 1) % 2

    def send_tiles(parity):
        for dy, dz in NEAR[::-1] + [(0, 0)]:
            for s in range(2):
                if (dy + dz + s) % 2 != parity or (s == 0 and (dy, dz) == (0, 0)):
                    continue
                ty, tz = (y + dy) % 4, (z + dz) % 4
                to_lo = lo if s == 0 else 1 - lo
                send(
                    packed.at[to_lo * 16 + tz * 4 + ty], placed.at[me], packed_send.at[0],
                    packed_recv.at[0], device(hi * 2 + to_lo, ty, tz, core),
                ).start()

    own_packed = pltpu.make_async_copy(packed.at[me], placed.at[me], own_sem.at[1])

    @pl.when(takes)
    def _():
        own_packed.start()
        send_tiles(0)

    @pl.when(jnp.logical_not(takes))
    def _():
        send_tiles(1)

    for copy in direct[FIRST:]:
        copy.start()

    for i in range(9, 15):
        onward_step(i)

    og_high, og_low = split(spread(dup, in_layer))

    def og_body(t, carry):
        cols = pl.ds(pl.multiple_of(t * TILE, TILE), TILE)
        bt_high, bt_low = basis_terms(cols)
        og[:, cols] = dot(og_high, bt_high) + (dot(og_high, bt_low) + dot(og_low, bt_high))
        return carry

    lax.fori_loop(0, D // TILE, og_body, 0)
    steps = {"side": side_step, "swap": swap_step}
    hand_over = send(placed, placed, packed_send.at[1], packed_recv.at[1], partner)
    tiles = [
        send(packed.at[pl.ds(0, n)], placed.at[pl.ds(0, n)], packed_send.at[0], packed_recv.at[0], up)
        for n in (15, 16, 31)
    ]
    late = 9
    for kind, i in PASSES[:-late]:
        steps[kind](i)

    @pl.when(takes)
    def _():
        own_packed.wait()
        tiles[2].wait_recv()
        hand_over.start()

    for kind, i in PASSES[-late:]:
        steps[kind](i)

    @pl.when(jnp.logical_not(takes))
    def _():
        hand_over.wait_recv()

    copies[10].wait()
    copies[11].wait()
    own_copy.wait()
    for i in range(32):
        send(r.at[0, 0], r.at[other, 0], swap_send, swap_recv.at[i], partner).wait_recv()

    flat = r.at[0]
    send(flat.at[pl.ds(0, 15)], flat.at[pl.ds(0, 15)], far_send, far_recv.at[0], up).wait_send()
    send(relay.at[pl.ds(0, 15)], relay.at[pl.ds(0, 15)], relay_send, far_recv.at[0], up).wait_send()
    send(flat.at[pl.ds(0, 16)], flat.at[pl.ds(0, 16)], side_send, far_recv.at[0], up).wait_send()
    send(flat, flat, swap_send, far_recv.at[0], up).wait_send()
    for copy in part_copies:
        copy.wait_send()

    @pl.when(takes)
    def _():
        tiles[0].wait_send()
        hand_over.wait_send()

    @pl.when(jnp.logical_not(takes))
    def _():
        tiles[1].wait_send()


def finish(
    w, m, r, og, placed, terms, table_v, new_weights, new_momentum, replica,
    moved_w, moved_m, rows, table, sem, row_sem, table_sem,
):
    table_copy = pltpu.make_async_copy(table_v, table, table_sem)
    table_copy.start()
    got = placed[...].reshape(256, 128)
    got_turned = pltpu.roll(got, RANK, 1)
    lane = lax.broadcasted_iota(jnp.int32, (1, 128), 1)
    low = lane < RANK
    sides = []
    for j in range(2):
        pairs = jnp.where(low, got, got_turned) if j == 0 else jnp.where(low, got_turned, got)
        sides.append(jnp.concatenate(split(pairs), axis=1))

    copies = []

    def issue(k):
        for copy in copies[2 * k:2 * k + 2]:
            copy.start()

    def out_body(b, carry):
        slot = table[0, b]
        for half in range(2):
            cols = slice(half * HALF, (half + 1) * HALF)
            rows[b, :, cols] = r[half, slot // 2, slot % 2] - (
                outer_rate * (1.0 + momentum_decay)
            ) * og[pl.ds(pl.multiple_of(b * 8, 8), 8), cols]
        return carry

    row_copies = [
        pltpu.make_async_copy(rows.at[pl.ds(g * 8, 8)], replica.at[pl.ds(g * 8, 8)], row_sem.at[g])
        for g in range(4)
    ]
    for j in range(2):
        layer = jnp.sum(jnp.where(lane == 32 + j, table_v[...], 0))
        use = jnp.where(lane == 34 + j, table_v[...], 0)
        use = jnp.sum(use, axis=1, keepdims=True).astype(F32)
        for t in range(D // TILE):
            cols = slice(t * TILE, (t + 1) * TILE)
            k = j * (D // TILE) + t
            grad = dot(sides[j], terms[layer, :, cols])
            moved = (momentum_decay * m[j, :, :, :, :, cols].reshape(256, TILE) + grad) * use
            moved_m[j, :, cols] = moved
            moved_w[j, :, cols] = (
                w[j, :, :, :, :, cols].reshape(256, TILE)
                - outer_rate * (grad + momentum_decay * moved)
            ) * use
            copies.append(pltpu.make_async_copy(
                moved_m.at[j, :, cols], new_momentum.at[j, :, cols], sem.at[0, k]))
            copies.append(pltpu.make_async_copy(
                moved_w.at[j, :, cols], new_weights.at[j, :, cols], sem.at[1, k]))
            if k > 0:
                issue(k - 1)
            if k in GROUP_AT:
                g = GROUP_AT.index(k)
                if g == 0:
                    table_copy.wait()
                else:
                    row_copies[g - 1].start()
                lax.fori_loop(g * 8, g * 8 + 8, out_body, 0)
    issue(2 * (D // TILE) - 1)

    row_copies[3].start()
    for copy in copies + row_copies:
        copy.wait()


def local(replica_delta, layer_basis, layer_of, owner_of, weights_owned, momentum_owned):
    vmem = pl.BlockSpec(memory_space=pltpu.VMEM)
    hbm = pl.BlockSpec(memory_space=pltpu.HBM)
    dma = pltpu.SemaphoreType.DMA
    basis = jnp.swapaxes(layer_basis, 1, 2)
    delta = replica_delta.reshape(256, D)
    weights = weights_owned.reshape(2, 2, 4, 4, 8, D)
    momentum = momentum_owned.reshape(2, 2, 4, 4, 8, D)
    between = pl.pallas_call(
        exchange,
        out_shape=(
            pltpu.VMEM((2, 2, 4, 4, 8, D), F32),
            pltpu.VMEM((2, 2, 4, 4, 8, D), F32),
            pltpu.VMEM((2, OWN, 2, 8, HALF), F32),
            pltpu.VMEM((256, D), F32),
            pltpu.VMEM((OWN, 8, 128), F32),
            pltpu.VMEM((4, 4 * RANK, D), BF16),
            pltpu.VMEM((1, 128), jnp.int32),
        ),
        in_specs=[hbm] * 6,
        out_specs=(vmem,) * 7,
        scratch_shapes=[
            pltpu.VMEM((1, BLOCKS), jnp.int32),
            pltpu.VMEM((1, BLOCKS), jnp.int32),
            pltpu.VMEM((256, D), F32),
            pltpu.VMEM((4, RANK, D), F32),
            pltpu.VMEM((2, 4, 4, 2, 8, HALF), F32),
            pltpu.VMEM((16, 8, HALF), F32),
            pltpu.VMEM((4, 128, 128), F32),
            pltpu.VMEM((OWN, 8, 128), F32),
            dma((12,)),
            dma, dma((15,)),
            dma, dma((15,)),
            dma, dma((2, 16)),
            dma, dma((32,)),
            dma((3,)), dma((3,)),
            dma((2,)), dma((2,)),
            dma((2,)),
            dma((2,)),
        ],
        compiler_params=pltpu.CompilerParams(
            collective_id=0, has_side_effects=True, vmem_limit_bytes=45 << 20
        ),
        name="outer_step",
    )(owner_of.reshape(1, BLOCKS), layer_of.reshape(1, BLOCKS), delta, basis, weights, momentum)
    shapes = ((2, 256, D), (2, 256, D), (BLOCKS, 8, D))
    return pl.pallas_call(
        finish,
        out_shape=tuple(jax.ShapeDtypeStruct(shape, F32) for shape in shapes),
        in_specs=[vmem] * 7,
        out_specs=(hbm,) * 3,
        scratch_shapes=[
            pltpu.VMEM((2, 256, D), F32), pltpu.VMEM((2, 256, D), F32),
            pltpu.VMEM((BLOCKS, 8, D), F32), pltpu.SMEM((1, 128), jnp.int32),
            dma((2, 14)), dma((4,)), dma,
        ],
        compiler_params=pltpu.CompilerParams(vmem_limit_bytes=16 << 20),
        name="finish",
    )(*between)


def solution(mesh):
    placed = (
        P("rep", None, "own", None),
        P(),
        P(),
        P(),
        P("own", None, None),
        P("own", None, None),
    )
    return jax.shard_map(
        local,
        mesh=mesh,
        in_specs=placed,
        out_specs=(P("own", None, None), P("own", None, None), P(None, "own", None)),
        check_vma=False,
    )
```
